256 devices in a mesh: frame: 8 (over z_lo, x), brick: 32 (over y, z_hi, core).
Axes of the slice: x: 4, y: 4, z: 8 (z_hi: 4, z_lo: 2; z = z_hi * 2 + z_lo), core: 2. Of those that a mesh axis runs over, the one named last changes fastest.
Arguments:
- intensity: float32 [32, 512, 128], P('frame', 'brick'), may hold values from 0.1 to 10
- correction: float32 [32, 512, 128], P('frame', 'brick'), may hold values from 0.3 to 3
- splitting: bfloat16 [32, 32, 8, 128, 512], P('frame', 'brick'), may hold values from 0 to 0.015625
- block_count: int32 [32, 32], P('frame', 'brick'), may hold values from 1 to 8, 128 in all within a row
- pix_index: int32 [32, 32, 8], P('frame', 'brick'), may hold values from 0 to 511, as said below
- vox_offset: int32 [32, 32, 8], P('frame', 'brick'), may hold values from 0 to 129
Outputs:
- merged: float32 [32, 128, 512], P('brick', 'frame')
- weight: float32 [32, 128, 512], P('brick', 'frame')
The draws below stay inside these ranges and needn't reach their ends.
Inputs may be any that keep to these rules, and one draw needn't show every extreme that they name: `block_count`: each frame's counts over the bricks sum to 128, and some pair of the frame holds 8. `pix_index`: the 32 slots of one device (its frames, its brick, padded slots included) include at most 4 slots (counted with repeats, over all of the device's frames) whose pixel block lies in the range 16 * c to 16 * c + 15, for every c; on every device some c has exactly 4 such slots.
All inputs are finite; a program needn't handle non-finite values. No bound on the sum of `block_count` on one device may be relied on, other than what follows from the above.
Results may differ from the reference program's by a relative error of at most 0.00049.
Values may be sent and summed in bfloat16 or wider, within the bound.
A program may use at most 64 MiB of HBM per device.

```python
import math
import jax
import jax.numpy as jnp
import numpy as np
from jax import lax

P_SIZE = 128
V = 512
FR_DEV = 4
MAXB = 8
PB_DEV = 16
CAP = 4
FRAMES = 32
BRICKS = 32
PBLK = 512
BLK = 128


def draw_pix_index(key, part):
    frame_groups = FRAMES // FR_DEV
    slot_count = FR_DEV * MAXB
    subkeys = jax.random.split(key, frame_groups * BRICKS)

    def draw_device(device_key):
        key_top, key_pool, key_order, key_resident = jax.random.split(device_key, 4)
        top_owner = jax.random.randint(key_top, (), 0, BRICKS, dtype=jnp.int32)
        shuffled = jax.random.permutation(key_pool, (BRICKS - 1) * (CAP - 1))[:slot_count - CAP].astype(jnp.int32)
        others = shuffled // (CAP - 1)
        others = jnp.where(others >= top_owner, others + 1, others)
        owners = jnp.concatenate([jnp.full((CAP,), top_owner, dtype=jnp.int32), others])
        owners = jax.random.permutation(key_order, owners)
        local_block = jax.random.randint(key_resident, (slot_count,), 0, PB_DEV, dtype=jnp.int32)
        return owners * PB_DEV + local_block
    drawn = jax.vmap(draw_device)(subkeys)
    drawn = drawn.reshape(frame_groups, BRICKS, FR_DEV, MAXB)
    return jnp.transpose(drawn, (0, 2, 1, 3)).reshape(FRAMES, BRICKS, MAXB)


def plant(values, rng, low, top_value):
    extent = values.shape
    index_at = [jax.random.randint(jax.random.fold_in(rng, axis), (), 0, extent[axis]) for axis in range(len(extent))]
    values = values.at[tuple(index_at)].set(low)
    longest = extent.index(max(extent))
    index_at[longest] = (index_at[longest] + 1) % extent[longest]
    return values.at[tuple(index_at)].set(top_value)


def steps_of(rng, shape, pieces, low, largest):
    def one(dim, blocks):
        steps = jax.random.uniform(jax.random.fold_in(jax.random.fold_in(rng, 6), dim), (blocks,), jnp.float32, low / len(pieces), largest / len(pieces))
        return jnp.repeat(jnp.exp(steps), shape[dim] // blocks).reshape((-1,) + (1,) * (len(shape) - dim - 1))

    gain = one(*pieces[0])
    for cut in pieces[1:]:
        gain = gain * one(*cut)
    return gain


def profile(count, total, limit, skew):
    portions = [(1 << 20) // math.isqrt(rank ** skew) + 1 for rank in range(2, count + 1)]
    surplus, holding = total - limit - (count - 1), [1] * (count - 1)
    while surplus > 0:
        free = [i for i in range(count - 1) if holding[i] < limit]
        whole, remaining = sum([portions[i] for i in free]), surplus
        for i in free:
            extra = min(limit - holding[i], max(1, remaining * portions[i] // whole), surplus)
            holding[i] = holding[i] + extra
            surplus = surplus - extra
    return np.array([limit] + holding)


def uneven_parts(rng, count, total, limit, skew):
    if count == 2:
        one = jax.random.randint(rng, (), max(1, total - limit), min(limit, total - 1) + 1)
        return jnp.stack([one, total - one])
    lengths = jnp.asarray(profile(count, total, limit, skew), jnp.int32)
    pairs = (count - 1) // 2
    source_of, sink = lengths[1:1 + 2 * pairs:2], lengths[2:2 + 2 * pairs:2]
    room = jnp.minimum(source_of - 1, limit - sink)
    moved = jax.random.randint(jax.random.fold_in(rng, 1), (pairs,), 0, 1 << 20) % (room + 1)
    lengths = lengths.at[1:1 + 2 * pairs:2].set(source_of - moved).at[2:2 + 2 * pairs:2].set(sink + moved)
    return lengths[jax.random.permutation(jax.random.fold_in(rng, 2), count)]


def setup_inputs(seed: int = 0) -> dict:
    arg_keys = jax.random.split(jax.random.key(seed), 7)
    return {
        "intensity": jnp.clip(jnp.exp(math.log(10.0) - 4.6051702 * jax.random.uniform(arg_keys[0], (FRAMES, PBLK, P_SIZE), jnp.float32) ** steps_of(arg_keys[0], (FRAMES, PBLK, P_SIZE), ((0, 8), (1, 32)), -0.2, 0.2)), 0.1, 10.0),
        "correction": jnp.clip(jnp.exp(math.log(3.0) - 2.3025851 * jax.random.uniform(arg_keys[1], (FRAMES, PBLK, P_SIZE), jnp.float32) ** steps_of(arg_keys[1], (FRAMES, PBLK, P_SIZE), ((0, 8), (1, 32)), -0.2, 0.2)), 0.3, 3.0),
        "splitting": jnp.clip(0.015625 * jax.random.uniform(arg_keys[2], (FRAMES, BRICKS, MAXB, P_SIZE, V), jnp.float32) ** steps_of(arg_keys[2], (FRAMES, BRICKS, MAXB, P_SIZE, V), ((0, 8), (1, 32)), -0.2, 0.2), 0.0, 0.015625).astype(jnp.bfloat16),
        "block_count": jax.vmap(lambda own: uneven_parts(own, BRICKS, BRICKS * MAXB // 2, MAXB, 2))(jax.random.split(arg_keys[3], FRAMES)).reshape((FRAMES, BRICKS)).astype(jnp.int32),
        "pix_index": draw_pix_index(jax.random.fold_in(arg_keys[6], 71), 0),
        "vox_offset": plant(jax.random.randint(arg_keys[5], (FRAMES, BRICKS, MAXB), 0, BLK + 2), jax.random.fold_in(arg_keys[5], 1), 0, (BLK + 2) - 1).astype(jnp.int32),
    }


def reference(intensity, correction, splitting, block_count, pix_index, vox_offset):
    detector_pixel_rows = jnp.stack([intensity, correction], axis=2).astype(jnp.bfloat16)
    row_total = BRICKS * BLK
    brick_base = (jnp.arange(BRICKS, dtype=jnp.int32) * BLK)[:, None]
    slot_ids = jnp.arange(MAXB, dtype=jnp.int32)[None, :]

    def add_frame(totals, inputs):
        frame_rows, frame_split, counts, indices, offsets = inputs
        picked = frame_rows[indices]
        contrib = jnp.einsum("bmck,bmkv->bmcv", picked.astype(jnp.float32), frame_split.astype(jnp.float32), precision=lax.Precision.HIGHEST)
        target = brick_base + offsets - 1
        keep_mask = (slot_ids < counts[:, None]) & (target >= 0) & (target < row_total)
        contrib = jnp.where(keep_mask[:, :, None, None], contrib, jnp.float32(0.0))
        target = jnp.clip(target, 0, row_total - 1).astype(jnp.int32)
        totals = totals.at[target.reshape(-1)].add(contrib.reshape(BRICKS * MAXB, 2, V))
        return totals, jnp.float32(0.0)

    start = jnp.zeros((row_total, 2, V), jnp.float32)
    totals, unused = lax.scan(add_frame, start, (detector_pixel_rows, splitting, block_count, pix_index, vox_offset))
    weight = totals[:, 1].reshape(BRICKS, BLK, V)
    merged = totals[:, 0].reshape(BRICKS, BLK, V) / jnp.maximum(weight, 1.0)
    return merged, weight
```

```python
import functools

import jax
import jax.numpy as jnp
from jax import lax
from jax.experimental import pallas as pl
from jax.experimental.pallas import tpu as pltpu
from jax.sharding import PartitionSpec as P

MESH = pl.DeviceIdType.MESH
CAP = 4
FR_DEV = 4
MAXB = 8
PB_DEV = 16
ROWS_DEV = 16
SLOTS = FR_DEV * MAXB
PIX = 128
VOX = 512
HALVES = 2
WIDTH = VOX // HALVES
CHUNKS = 4


def iota(shape, dim):
    return lax.broadcasted_iota(jnp.int32, shape, dim)


def kernel(
    bricks,
    groups,
    pix_ref,
    vox_ref,
    count_ref,
    intensity_hbm,
    correction_hbm,
    split_hbm,
    merged_ref,
    weight_ref,
    inten,
    corr,
    split,
    request,
    packed,
    received,
    rowbuf,
    lhs,
    acc,
    partial,
    total,
    over_send,
    over_recv,
    load_sem,
    split_sem,
    req_send,
    req_recv,
    data_send,
    data_recv,
    sum_send,
    sum_recv,
    low_send,
    high_send,
    over_sem,
):
    me_f = lax.axis_index("frame")
    me_b = lax.axis_index("brick")
    barrier = pltpu.get_barrier_semaphore()

    def brick_peer(i):
        return lax.rem(me_b + i, bricks)

    def frame_peer(i):
        return lax.rem(me_f + i, groups)

    def greet_brick(i, carry):
        pl.semaphore_signal(
            barrier, inc=1, device_id={"brick": brick_peer(i)}, device_id_type=MESH
        )
        return carry

    def greet_frame(i, carry):
        pl.semaphore_signal(
            barrier, inc=1, device_id={"frame": frame_peer(i)}, device_id_type=MESH
        )
        return carry

    lax.fori_loop(1, bricks, greet_brick, 0)
    lax.fori_loop(1, groups, greet_frame, 0)

    loads = [
        pltpu.make_async_copy(intensity_hbm, inten, load_sem.at[0]),
        pltpu.make_async_copy(correction_hbm, corr, load_sem.at[1]),
    ]
    depth = SLOTS * PIX // CHUNKS
    splits = [
        pltpu.make_async_copy(
            split_hbm.at[pl.ds(k * depth, depth)],
            split.at[pl.ds(k * depth, depth)],
            split_sem.at[k],
        )
        for k in range(CHUNKS)
    ]
    for copy in loads + splits:
        copy.start()

    lane = iota((1, PIX), 1)
    row = jnp.full((1, PIX), -1, jnp.int32)
    for s in range(SLOTS):
        row = jnp.where(lane == s, pix_ref[s // MAXB, 0, s % MAXB], row)
    sub2, lane2 = iota((SLOTS, PIX), 0), iota((SLOTS, PIX), 1)
    column = jnp.sum(
        jnp.where(sub2 == lane2, jnp.broadcast_to(row, (SLOTS, PIX)), 0), axis=1, keepdims=True
    )
    same = (jnp.broadcast_to(row >> 4, (SLOTS, PIX)) == (column >> 4)).astype(jnp.int32)
    rank_row = jnp.sum(jnp.where(sub2 < lane2, same, 0), axis=0, keepdims=True)
    rank_col = jnp.sum(jnp.where(lane2 < sub2, same, 0), axis=1, keepdims=True)
    code = ((row >> 4) * CAP + rank_row) * 64 + (lane >> 3) * PB_DEV + (row & 15)
    request[me_b] = jnp.where(lane < SLOTS, code, -1)
    key = (column >> 4) * CAP + rank_col
    wide = iota((SLOTS, bricks * 2 * CAP), 1)
    pick = jnp.concatenate(
        [
            jnp.where(wide == key * 2 + c, 1.0, 0.0).astype(jnp.float32)
            for c in range(2)
        ],
        axis=0,
    ).astype(jnp.bfloat16)

    pl.semaphore_wait(barrier, bricks - 1 + groups - 1)

    def send_request(i, carry):
        pltpu.make_async_remote_copy(
            src_ref=request.at[me_b],
            dst_ref=request.at[me_b],
            send_sem=req_send,
            recv_sem=req_recv,
            device_id={"brick": brick_peer(i)},
            device_id_type=MESH,
        ).start()
        return carry

    lax.fori_loop(1, bricks, send_request, 0)

    for copy in loads:
        copy.wait()
    own = jnp.concatenate(
        [inten[...].reshape(FR_DEV * PB_DEV, PIX), corr[...].reshape(FR_DEV * PB_DEV, PIX)],
        axis=0,
    ).astype(jnp.bfloat16)

    def all_of(buffer, sem):
        others = buffer.at[pl.ds(0, bricks - 1)]
        return pltpu.make_async_copy(others, others, sem)

    all_of(request, req_recv).wait()

    asked = jnp.broadcast_to(request[...], (bricks, 2 * CAP, PIX))
    place = iota((bricks, 2 * CAP, PIX), 1)
    lane3 = iota((bricks, 2 * CAP, PIX), 2)
    wanted = (asked >> 6) == me_b * CAP + (place >> 1)
    found = jnp.sum(jnp.where(wanted, (asked & 63) + 1, 0), axis=2, keepdims=True)
    chosen = jnp.where(
        (found > 0) & (lane3 == (place & 1) * 64 + found - 1), 1.0, 0.0
    ).astype(jnp.float32)
    select = chosen.reshape(bricks * 2 * CAP, PIX).astype(jnp.bfloat16)
    blocks = jnp.dot(select, own, preferred_element_type=jnp.float32)
    packed[...] = blocks.reshape(bricks, 2 * CAP, PIX).astype(jnp.bfloat16)

    def send_data(i, carry):
        peer = brick_peer(i)
        pltpu.make_async_remote_copy(
            src_ref=packed.at[peer],
            dst_ref=received.at[me_b],
            send_sem=data_send,
            recv_sem=data_recv,
            device_id={"brick": peer},
            device_id_type=MESH,
        ).start()
        return carry

    lax.fori_loop(1, bricks, send_data, 0)
    received[me_b] = packed[me_b]
    all_of(received, data_recv).wait()

    table = received[...].astype(jnp.float32).reshape(bricks * 2 * CAP, PIX).astype(jnp.bfloat16)
    rowbuf[...] = jnp.dot(pick, table, preferred_element_type=jnp.float32)

    inner = groups * ROWS_DEV
    for copy in splits:
        copy.wait()

    def place_slot(f, m, carry):
        s = f * MAXB + m
        offset = vox_ref[f, 0, m]
        target = jnp.where(offset == 0, inner, jnp.where(offset == inner + 1, inner + 1, offset - 1))
        target = jnp.where(m < count_ref[f, 0], target, -1)
        hit = iota((inner + 8, PIX), 0) == target
        start = pl.multiple_of(s * PIX, PIX)
        parts = []
        for c in range(2):
            value = jnp.broadcast_to(rowbuf[pl.ds(c * SLOTS + s, 1), :], (inner + 8, PIX))
            parts.append(jnp.where(hit, value, 0.0))
        for g in range(groups):
            for c in range(2):
                lhs[pl.ds((2 * g + c) * ROWS_DEV, ROWS_DEV), pl.ds(start, PIX)] = parts[c][
                    g * ROWS_DEV : (g + 1) * ROWS_DEV
                ].astype(jnp.bfloat16)
        lhs[pl.ds(2 * inner, 16), pl.ds(start, PIX)] = jnp.concatenate(
            [part[inner:] for part in parts], axis=0
        ).astype(jnp.bfloat16)
        return carry

    def place_frame(f, carry):
        return lax.fori_loop(0, MAXB, functools.partial(place_slot, f), carry)

    lax.fori_loop(0, FR_DEV, place_frame, 0)

    def sum_copy(half, i):
        peer = frame_peer(i)
        return pltpu.make_async_remote_copy(
            src_ref=acc.at[half, pl.ds(peer * 2 * ROWS_DEV, 2 * ROWS_DEV)],
            dst_ref=partial.at[half, me_f],
            send_sem=sum_send.at[half],
            recv_sem=sum_recv.at[half],
            device_id={"frame": peer},
            device_id_type=MESH,
        )

    for half in range(HALVES):
        columns = pl.ds(half * WIDTH, WIDTH)
        acc[half] = jnp.dot(lhs[...], split[:, columns], preferred_element_type=jnp.float32)

        def send_sum(i, carry):
            sum_copy(half, i).start()
            return carry

        lax.fori_loop(1, groups, send_sum, 0)

    for side in range(2):
        for c in range(2):
            for n in range(VOX // PIX):
                half, at = n * PIX // WIDTH, n * PIX % WIDTH
                over_send[side, pl.ds(c * (VOX // PIX) + n, 1), :] = acc[
                    half, pl.ds(2 * inner + c * 8 + side, 1), pl.ds(at, PIX)
                ]

    def over_copy(side, step, owner, sem):
        return pltpu.make_async_remote_copy(
            src_ref=over_send.at[side],
            dst_ref=over_recv.at[me_f],
            send_sem=sem,
            recv_sem=over_sem,
            device_id={"frame": owner, "brick": brick_peer(step)},
            device_id_type=MESH,
        )

    low = over_copy(0, bricks - 1, groups - 1, low_send)
    high = over_copy(1, 1, 0, high_send)

    @pl.when(me_b > 0)
    def _():
        low.start()

    @pl.when(me_b < bricks - 1)
    def _():
        high.start()

    for half in range(HALVES):
        columns = pl.ds(half * WIDTH, WIDTH)
        others = partial.at[half, pl.ds(0, groups - 1)]
        partial[half, me_f] = acc[half, pl.ds(pl.multiple_of(me_f * 2 * ROWS_DEV, 32), 2 * ROWS_DEV), :]
        pltpu.make_async_copy(others, others, sum_recv.at[half]).wait()
        value = partial[half, 0]
        for g in range(1, groups):
            value = value + partial[half, g]
        total[:, columns] = value

    def take_overhang(at):
        pltpu.make_async_copy(over_recv, over_recv, over_sem).wait()
        value = over_recv[0]
        for g in range(1, groups):
            value = value + over_recv[g]
        for c in range(2):
            for n in range(VOX // PIX):
                where = (pl.ds(c * ROWS_DEV + at, 1), pl.ds(n * PIX, PIX))
                total[where] = total[where] + value[c * (VOX // PIX) + n : c * (VOX // PIX) + n + 1]

    @pl.when((me_f == groups - 1) & (me_b < bricks - 1))
    def _():
        take_overhang(ROWS_DEV - 1)

    @pl.when((me_f == 0) & (me_b > 0))
    def _():
        take_overhang(0)

    weight = total[pl.ds(ROWS_DEV, ROWS_DEV), :]
    weight_ref[...] = weight
    merged_ref[...] = total[pl.ds(0, ROWS_DEV), :] / jnp.maximum(weight, 1.0)

    all_of(request, req_send).wait()
    all_of(packed, data_send).wait()
    for half in range(HALVES):
        others = partial.at[half, pl.ds(0, groups - 1)]
        pltpu.make_async_copy(others, others, sum_send.at[half]).wait()

    @pl.when(me_b > 0)
    def _():
        low.wait_send()

    @pl.when(me_b < bricks - 1)
    def _():
        high.wait_send()


def on_device(intensity, correction, splitting, block_count, pix_index, vox_offset):
    bricks = lax.axis_size("brick")
    groups = lax.axis_size("frame")
    inner = groups * ROWS_DEV
    rows = 2 * inner + 16
    smem = pl.BlockSpec(memory_space=pltpu.SMEM)
    hbm = pl.BlockSpec(memory_space=pl.ANY)
    vmem = pl.BlockSpec(memory_space=pltpu.VMEM)
    dma = pltpu.SemaphoreType.DMA
    merged, weight = pl.pallas_call(
        functools.partial(kernel, bricks, groups),
        out_shape=[jax.ShapeDtypeStruct((ROWS_DEV, VOX), jnp.float32)] * 2,
        in_specs=[smem, smem, smem, hbm, hbm, hbm],
        out_specs=[vmem, vmem],
        scratch_shapes=[
            pltpu.VMEM((FR_DEV, PB_DEV, PIX), jnp.float32),
            pltpu.VMEM((FR_DEV, PB_DEV, PIX), jnp.float32),
            pltpu.VMEM((SLOTS * PIX, VOX), jnp.bfloat16),
            pltpu.VMEM((bricks, 1, PIX), jnp.int32),
            pltpu.VMEM((bricks, 2 * CAP, PIX), jnp.bfloat16),
            pltpu.VMEM((bricks, 2 * CAP, PIX), jnp.bfloat16),
            pltpu.VMEM((2 * SLOTS, PIX), jnp.float32),
            pltpu.VMEM((rows, SLOTS * PIX), jnp.bfloat16),
            pltpu.VMEM((HALVES, rows, WIDTH), jnp.float32),
            pltpu.VMEM((HALVES, groups, 2 * ROWS_DEV, WIDTH), jnp.float32),
            pltpu.VMEM((2 * ROWS_DEV, VOX), jnp.float32),
            pltpu.VMEM((2, 8, PIX), jnp.float32),
            pltpu.VMEM((groups, 8, PIX), jnp.float32),
            dma((2,)),
            dma((CHUNKS,)),
            dma,
            dma,
            dma,
            dma,
            dma((HALVES,)),
            dma((HALVES,)),
            dma,
            dma,
            dma,
        ],
        compiler_params=pltpu.CompilerParams(
            collective_id=0, has_side_effects=True, vmem_limit_bytes=32 * 1024 * 1024
        ),
    )(
        pix_index,
        vox_offset,
        block_count,
        intensity,
        correction,
        splitting.reshape(SLOTS * PIX, VOX),
    )
    return (merged[None], weight[None])


def solution(mesh):
    placed = (
        P("frame", "brick", None),
        P("frame", "brick", None),
        P("frame", "brick", None, None, None),
        P("frame", "brick"),
        P("frame", "brick", None),
        P("frame", "brick", None),
    )
    return jax.shard_map(
        on_device,
        mesh=mesh,
        in_specs=placed,
        out_specs=(P("brick", "frame", None), P("brick", "frame", None)),
        check_vma=False,
    )
```

```python
import functools

import jax
import jax.numpy as jnp
from jax import lax
from jax.experimental import pallas as pl
from jax.experimental.pallas import tpu as pltpu
from jax.sharding import PartitionSpec as P

MESH = pl.DeviceIdType.MESH
CAP = 4
FR_DEV = 4
MAXB = 8
PB_DEV = 16
ROWS_DEV = 16
SLOTS = FR_DEV * MAXB
PIX = 128
VOX = 512
HALVES = 2
WIDTH = VOX // HALVES
CHUNKS = 4
NEAR = 8


def iota(shape, dim):
    return lax.broadcasted_iota(jnp.int32, shape, dim)


def kernel(
    bricks,
    groups,
    pix_hbm,
    vox_hbm,
    count_hbm,
    intensity_hbm,
    correction_hbm,
    split_hbm,
    total,
    pix_ref,
    vox_ref,
    count_ref,
    inten,
    corr,
    split,
    pixels,
    request,
    packed,
    received,
    rowbuf,
    lhs,
    acc,
    partial,
    over_send,
    over_recv,
    load_sem,
    split_sem,
    pix_send,
    pix_recv,
    req_send,
    req_recv,
    data_send,
    data_recv,
    sum_send,
    sum_recv,
    over_send_sem,
    over_sem,
):
    me_f = lax.axis_index("frame")
    me_b = lax.axis_index("brick")
    far = bricks // NEAR
    me_far = me_b // NEAR
    me_near = me_b - me_far * NEAR
    held = CAP * far
    barrier = pltpu.get_barrier_semaphore()

    def brick_peer(i):
        return lax.rem(me_b + i, bricks)

    def near_index(i):
        return lax.rem(me_near + i, NEAR)

    def near_peer(i):
        return me_far * NEAR + near_index(i)

    def frame_peer(i):
        return lax.rem(me_f + i, groups)

    for i in range(1, far):
        pl.semaphore_signal(
            barrier, inc=1, device_id={"brick": brick_peer(i * NEAR)}, device_id_type=MESH
        )
    for i in range(1, NEAR):
        pl.semaphore_signal(
            barrier, inc=1, device_id={"brick": near_peer(i)}, device_id_type=MESH
        )
    for i in range(1, groups):
        pl.semaphore_signal(
            barrier, inc=1, device_id={"frame": frame_peer(i)}, device_id_type=MESH
        )

    tables = [
        pltpu.make_async_copy(pix_hbm, pix_ref, load_sem.at[0]),
        pltpu.make_async_copy(vox_hbm, vox_ref, load_sem.at[1]),
        pltpu.make_async_copy(count_hbm, count_ref, load_sem.at[2]),
    ]
    loads = [
        pltpu.make_async_copy(intensity_hbm, inten, load_sem.at[3]),
        pltpu.make_async_copy(correction_hbm, corr, load_sem.at[4]),
    ]
    depth = SLOTS * PIX // CHUNKS
    splits = [
        pltpu.make_async_copy(
            split_hbm.at[pl.ds(k * depth, depth)],
            split.at[pl.ds(k * depth, depth)],
            split_sem.at[k],
        )
        for k in range(CHUNKS)
    ]
    for copy in tables + loads + splits:
        copy.start()
    for copy in tables:
        copy.wait()

    lane = iota((1, PIX), 1)
    row = jnp.full((1, PIX), -1, jnp.int32)
    for s in range(SLOTS):
        row = jnp.where(lane == s, pix_ref[s // MAXB, 0, s % MAXB], row)
    sub2, lane2 = iota((SLOTS, PIX), 0), iota((SLOTS, PIX), 1)
    column = jnp.sum(
        jnp.where(sub2 == lane2, jnp.broadcast_to(row, (SLOTS, PIX)), 0), axis=1, keepdims=True
    )
    near_row = (row >> 4) & (NEAR - 1)
    near_col = (column >> 4) & (NEAR - 1)
    same = (jnp.broadcast_to(near_row, (SLOTS, PIX)) == near_col).astype(jnp.int32)
    rank_row = jnp.sum(jnp.where(sub2 < lane2, same, 0), axis=0, keepdims=True)
    rank_col = jnp.sum(jnp.where(lane2 < sub2, same, 0), axis=1, keepdims=True)
    where_row = (row // (NEAR * PB_DEV)) * 128 + (lane >> 3) * PB_DEV + (row & 15)
    code = (near_row * held + rank_row) * 1024 + where_row
    request[me_near] = jnp.where(lane < SLOTS, code, -1)
    key = near_col * held + rank_col
    wide = iota((SLOTS, NEAR * 2 * held), 1)
    pick = jnp.concatenate(
        [jnp.where(wide == key * 2 + c, 1.0, 0.0).astype(jnp.float32) for c in range(2)],
        axis=0,
    ).astype(jnp.bfloat16)

    for copy in loads:
        copy.wait()
    pixels[me_far] = jnp.concatenate(
        [inten[...].reshape(FR_DEV * PB_DEV, PIX), corr[...].reshape(FR_DEV * PB_DEV, PIX)],
        axis=0,
    ).astype(jnp.bfloat16)

    pl.semaphore_wait(barrier, far - 1 + NEAR - 1 + groups - 1)

    for i in range(1, far):
        pltpu.make_async_remote_copy(
            src_ref=pixels.at[me_far],
            dst_ref=pixels.at[me_far],
            send_sem=pix_send,
            recv_sem=pix_recv,
            device_id={"brick": brick_peer(i * NEAR)},
            device_id_type=MESH,
        ).start()
    for i in range(1, NEAR):
        pltpu.make_async_remote_copy(
            src_ref=request.at[me_near],
            dst_ref=request.at[me_near],
            send_sem=req_send,
            recv_sem=req_recv,
            device_id={"brick": near_peer(i)},
            device_id_type=MESH,
        ).start()

    def others_of(buffer, count, sem):
        others = buffer.at[pl.ds(0, count - 1)]
        return pltpu.make_async_copy(others, others, sem)

    others_of(request, NEAR, req_recv).wait()

    asked = jnp.concatenate(
        [jnp.broadcast_to(request[d], (2 * held, PIX)) for d in range(NEAR)], axis=0
    )
    place = lax.rem(iota((NEAR * 2 * held, PIX), 0), 2 * held)
    wanted = (asked >> 10) == me_near * held + (place >> 1)
    found = jnp.sum(jnp.where(wanted, (asked & 1023) + 1, 0), axis=1, keepdims=True)
    spot = jnp.where(found > 0, found - 1 + (place[:, 0:1] & 1) * 64, -1)
    select = jnp.where(iota((NEAR * 2 * held, far * PIX), 1) == spot, 1.0, 0.0)
    select = select.astype(jnp.float32).astype(jnp.bfloat16)

    others_of(pixels, far, pix_recv).wait()
    blocks = jnp.dot(
        select, pixels[...].reshape(far * PIX, PIX), preferred_element_type=jnp.float32
    ).astype(jnp.bfloat16)
    packed[...] = blocks.reshape(NEAR, 2 * held, PIX)

    for i in range(1, NEAR):
        pltpu.make_async_remote_copy(
            src_ref=packed.at[near_index(i)],
            dst_ref=received.at[me_near],
            send_sem=data_send,
            recv_sem=data_recv,
            device_id={"brick": near_peer(i)},
            device_id_type=MESH,
        ).start()
    received[me_near] = packed[me_near]
    others_of(received, NEAR, data_recv).wait()

    rowbuf[...] = jnp.dot(
        pick, received[...].reshape(NEAR * 2 * held, PIX), preferred_element_type=jnp.float32
    )

    inner = groups * ROWS_DEV

    def place_slot(f, m, carry):
        s = f * MAXB + m
        offset = vox_ref[f, 0, m]
        target = jnp.where(offset == 0, inner, jnp.where(offset == inner + 1, inner + 1, offset - 1))
        target = jnp.where(m < count_ref[f], target, -1)
        hit = iota((inner + 8, PIX), 0) == target
        start = pl.multiple_of(s * PIX, PIX)
        parts = []
        for c in range(2):
            value = jnp.broadcast_to(rowbuf[pl.ds(c * SLOTS + s, 1), :], (inner + 8, PIX))
            parts.append(jnp.where(hit, value, 0.0))
        for g in range(groups):
            for c in range(2):
                lhs[pl.ds((2 * g + c) * ROWS_DEV, ROWS_DEV), pl.ds(start, PIX)] = parts[c][
                    g * ROWS_DEV : (g + 1) * ROWS_DEV
                ].astype(jnp.bfloat16)
        lhs[pl.ds(2 * inner, 16), pl.ds(start, PIX)] = jnp.concatenate(
            [part[inner:] for part in parts], axis=0
        ).astype(jnp.bfloat16)
        return carry

    def place_frame(f, carry):
        return lax.fori_loop(0, MAXB, functools.partial(place_slot, f), carry)

    lax.fori_loop(0, FR_DEV, place_frame, 0)
    for copy in splits:
        copy.wait()

    def over_copy(side, half, step, owner):
        return pltpu.make_async_remote_copy(
            src_ref=over_send.at[side, half],
            dst_ref=over_recv.at[half, me_f],
            send_sem=over_send_sem.at[side],
            recv_sem=over_sem,
            device_id={"frame": owner, "brick": brick_peer(step)},
            device_id_type=MESH,
        )

    parts = WIDTH // PIX
    for half in range(HALVES):
        columns = pl.ds(half * WIDTH, WIDTH)
        acc[half] = jnp.dot(lhs[...], split[:, columns], preferred_element_type=jnp.float32)

        for side in range(2):
            for c in range(2):
                for n in range(parts):
                    over_send[side, half, pl.ds(c * parts + n, 1), :] = acc[
                        half, pl.ds(2 * inner + c * 8 + side, 1), pl.ds(n * PIX, PIX)
                    ]

        @pl.when(me_b > 0)
        def _():
            over_copy(0, half, bricks - 1, groups - 1).start()

        @pl.when(me_b < bricks - 1)
        def _():
            over_copy(1, half, 1, 0).start()

        for i in range(1, groups):
            peer = frame_peer(i)
            pltpu.make_async_remote_copy(
                src_ref=acc.at[half, pl.ds(peer * 2 * ROWS_DEV, 2 * ROWS_DEV)],
                dst_ref=partial.at[half, me_f],
                send_sem=sum_send.at[half],
                recv_sem=sum_recv.at[half],
                device_id={"frame": peer},
                device_id_type=MESH,
            ).start()
        partial[half, me_f] = acc[
            half, pl.ds(pl.multiple_of(me_f * 2 * ROWS_DEV, 2 * ROWS_DEV), 2 * ROWS_DEV), :
        ]

    for half in range(HALVES):
        columns = pl.ds(half * WIDTH, WIDTH)
        others = partial.at[half, pl.ds(0, groups - 1)]
        pltpu.make_async_copy(others, others, sum_recv.at[half]).wait()
        value = partial[half, 0]
        for g in range(1, groups):
            value = value + partial[half, g]
        total[:, columns] = value

    def take_overhang(at):
        pltpu.make_async_copy(over_recv, over_recv, over_sem).wait()
        for half in range(HALVES):
            value = over_recv[half, 0]
            for g in range(1, groups):
                value = value + over_recv[half, g]
            for c in range(2):
                for n in range(parts):
                    where = (pl.ds(c * ROWS_DEV + at, 1), pl.ds(half * WIDTH + n * PIX, PIX))
                    total[where] = total[where] + value[c * parts + n : c * parts + n + 1]

    @pl.when((me_f == groups - 1) & (me_b < bricks - 1))
    def _():
        take_overhang(ROWS_DEV - 1)

    @pl.when((me_f == 0) & (me_b > 0))
    def _():
        take_overhang(0)

    others_of(pixels, far, pix_send).wait()
    others_of(request, NEAR, req_send).wait()
    others_of(packed, NEAR, data_send).wait()
    for half in range(HALVES):
        others = partial.at[half, pl.ds(0, groups - 1)]
        pltpu.make_async_copy(others, others, sum_send.at[half]).wait()

    def sent_over(side):
        pltpu.make_async_copy(over_send.at[side], over_send.at[side], over_send_sem.at[side]).wait()

    @pl.when(me_b > 0)
    def _():
        sent_over(0)

    @pl.when(me_b < bricks - 1)
    def _():
        sent_over(1)


def on_device(intensity, correction, splitting, block_count, pix_index, vox_offset):
    bricks = lax.axis_size("brick")
    groups = lax.axis_size("frame")
    far = bricks // NEAR
    message = 2 * CAP * far
    rows = 2 * groups * ROWS_DEV + 16
    hbm = pl.BlockSpec(memory_space=pltpu.HBM)
    dma = pltpu.SemaphoreType.DMA
    total = pl.pallas_call(
        functools.partial(kernel, bricks, groups),
        out_shape=jax.ShapeDtypeStruct((2 * ROWS_DEV, VOX), jnp.float32),
        in_specs=[hbm] * 6,
        out_specs=pl.BlockSpec(memory_space=pltpu.VMEM),
        scratch_shapes=[
            pltpu.SMEM((FR_DEV, 1, MAXB), jnp.int32),
            pltpu.SMEM((FR_DEV, 1, MAXB), jnp.int32),
            pltpu.SMEM((FR_DEV,), jnp.int32),
            pltpu.VMEM((FR_DEV, PB_DEV, PIX), jnp.float32),
            pltpu.VMEM((FR_DEV, PB_DEV, PIX), jnp.float32),
            pltpu.VMEM((SLOTS * PIX, VOX), jnp.bfloat16),
            pltpu.VMEM((far, 2 * FR_DEV * PB_DEV, PIX), jnp.bfloat16),
            pltpu.VMEM((NEAR, 1, PIX), jnp.int32),
            pltpu.VMEM((NEAR, message, PIX), jnp.bfloat16),
            pltpu.VMEM((NEAR, message, PIX), jnp.bfloat16),
            pltpu.VMEM((2 * SLOTS, PIX), jnp.float32),
            pltpu.VMEM((rows, SLOTS * PIX), jnp.bfloat16),
            pltpu.VMEM((HALVES, rows, WIDTH), jnp.float32),
            pltpu.VMEM((HALVES, groups, 2 * ROWS_DEV, WIDTH), jnp.float32),
            pltpu.VMEM((2, HALVES, 2 * WIDTH // PIX, PIX), jnp.float32),
            pltpu.VMEM((HALVES, groups, 2 * WIDTH // PIX, PIX), jnp.float32),
            dma((5,)),
            dma((CHUNKS,)),
            dma,
            dma,
            dma,
            dma,
            dma,
            dma,
            dma((HALVES,)),
            dma((HALVES,)),
            dma((2,)),
            dma,
        ],
        compiler_params=pltpu.CompilerParams(
            collective_id=0, has_side_effects=True, vmem_limit_bytes=60 * 1024 * 1024
        ),
    )(
        pix_index,
        vox_offset,
        block_count.reshape(FR_DEV),
        intensity,
        correction,
        splitting.reshape(SLOTS * PIX, VOX),
    )
    weight = total[ROWS_DEV:]
    merged = total[:ROWS_DEV] / jnp.maximum(weight, 1.0)
    return (merged[None], weight[None])


def solution(mesh):
    placed = (
        P("frame", "brick", None),
        P("frame", "brick", None),
        P("frame", "brick", None, None, None),
        P("frame", "brick"),
        P("frame", "brick", None),
        P("frame", "brick", None),
    )
    return jax.shard_map(
        on_device,
        mesh=mesh,
        in_specs=placed,
        out_specs=(P("brick", "frame", None), P("brick", "frame", None)),
        check_vma=False,
    )
```

```python
import functools

import jax
import jax.numpy as jnp
from jax import lax
from jax.experimental import pallas as pl
from jax.experimental.pallas import tpu as pltpu
from jax.sharding import PartitionSpec as P

MESH = pl.DeviceIdType.MESH
CAP = 4
FR_DEV = 4
MAXB = 8
PB_DEV = 16
ROWS_DEV = 16
SLOTS = FR_DEV * MAXB
PIX = 128
VOX = 512
HALVES = 2
WIDTH = VOX // HALVES
CHUNKS = 4
FAR = 4


def iota(shape, dim):
    return lax.broadcasted_iota(jnp.int32, shape, dim)


def kernel(
    bricks,
    groups,
    pix_hbm,
    vox_hbm,
    count_hbm,
    intensity_hbm,
    correction_hbm,
    split_hbm,
    total,
    pix_ref,
    vox_ref,
    count_ref,
    inten,
    corr,
    split,
    pixels,
    request,
    packed,
    received,
    rowbuf,
    lhs,
    acc,
    partial,
    over_send,
    over_recv,
    load_sem,
    split_sem,
    pix_send,
    pix_recv,
    req_send,
    req_recv,
    data_send,
    data_recv,
    sum_send,
    sum_recv,
    over_send_sem,
    over_sem,
):
    me_f = lax.axis_index("frame")
    me_b = lax.axis_index("brick")
    near = bricks // FAR
    me_y = me_b // (2 * FAR)
    me_c = lax.rem(me_b, 2)
    me_far = lax.rem(me_b // 2, FAR)
    me_near = me_y * 2 + me_c
    held = CAP * FAR
    barrier = pltpu.get_barrier_semaphore()

    def brick_peer(i):
        return lax.rem(me_b + i, bricks)

    def brick_of(at_near, at_far):
        return (at_near // 2 * FAR + at_far) * 2 + lax.rem(at_near, 2)

    def near_index(i):
        return lax.rem(me_near + i, near)

    def near_peer(i):
        return brick_of(near_index(i), me_far)

    def far_peer(i):
        return brick_of(me_near, lax.rem(me_far + i, FAR))

    def frame_peer(i):
        return lax.rem(me_f + i, groups)

    for i in range(1, FAR):
        pl.semaphore_signal(
            barrier, inc=1, device_id={"brick": far_peer(i)}, device_id_type=MESH
        )
    for i in range(1, near):
        pl.semaphore_signal(
            barrier, inc=1, device_id={"brick": near_peer(i)}, device_id_type=MESH
        )
    for i in range(1, groups):
        pl.semaphore_signal(
            barrier, inc=1, device_id={"frame": frame_peer(i)}, device_id_type=MESH
        )

    tables = [
        pltpu.make_async_copy(pix_hbm, pix_ref, load_sem.at[0]),
        pltpu.make_async_copy(vox_hbm, vox_ref, load_sem.at[1]),
        pltpu.make_async_copy(count_hbm, count_ref, load_sem.at[2]),
    ]
    loads = [
        pltpu.make_async_copy(intensity_hbm, inten, load_sem.at[3]),
        pltpu.make_async_copy(correction_hbm, corr, load_sem.at[4]),
    ]
    depth = SLOTS * PIX // CHUNKS
    splits = [
        pltpu.make_async_copy(
            split_hbm.at[pl.ds(k * depth, depth)],
            split.at[pl.ds(k * depth, depth)],
            split_sem.at[k],
        )
        for k in range(CHUNKS)
    ]
    for copy in tables + loads + splits:
        copy.start()
    for copy in tables:
        copy.wait()

    lane = iota((1, PIX), 1)
    row = jnp.full((1, PIX), -1, jnp.int32)
    for s in range(SLOTS):
        row = jnp.where(lane == s, pix_ref[s // MAXB, 0, s % MAXB], row)
    sub2, lane2 = iota((SLOTS, PIX), 0), iota((SLOTS, PIX), 1)
    column = jnp.sum(
        jnp.where(sub2 == lane2, jnp.broadcast_to(row, (SLOTS, PIX)), 0), axis=1, keepdims=True
    )
    near_row = (row // (2 * FAR * PB_DEV)) * 2 + ((row >> 4) & 1)
    near_col = (column // (2 * FAR * PB_DEV)) * 2 + ((column >> 4) & 1)
    same = (jnp.broadcast_to(near_row, (SLOTS, PIX)) == near_col).astype(jnp.int32)
    rank_row = jnp.sum(jnp.where(sub2 < lane2, same, 0), axis=0, keepdims=True)
    rank_col = jnp.sum(jnp.where(lane2 < sub2, same, 0), axis=1, keepdims=True)
    where_row = ((row >> 5) & (FAR - 1)) * 128 + (lane >> 3) * PB_DEV + (row & 15)
    code = (near_row * held + rank_row) * 1024 + where_row
    request[me_near] = jnp.where(lane < SLOTS, code, -1)
    key = near_col * held + rank_col
    wide = iota((SLOTS, near * 2 * held), 1)
    pick = jnp.concatenate(
        [jnp.where(wide == key * 2 + c, 1.0, 0.0).astype(jnp.float32) for c in range(2)],
        axis=0,
    ).astype(jnp.bfloat16)

    for copy in loads:
        copy.wait()
    pixels[me_far] = jnp.concatenate(
        [inten[...].reshape(FR_DEV * PB_DEV, PIX), corr[...].reshape(FR_DEV * PB_DEV, PIX)],
        axis=0,
    ).astype(jnp.bfloat16)

    pl.semaphore_wait(barrier, FAR - 1 + near - 1 + groups - 1)

    for i in range(1, FAR):
        pltpu.make_async_remote_copy(
            src_ref=pixels.at[me_far],
            dst_ref=pixels.at[me_far],
            send_sem=pix_send,
            recv_sem=pix_recv,
            device_id={"brick": far_peer(i)},
            device_id_type=MESH,
        ).start()
    for i in range(1, near):
        pltpu.make_async_remote_copy(
            src_ref=request.at[me_near],
            dst_ref=request.at[me_near],
            send_sem=req_send,
            recv_sem=req_recv,
            device_id={"brick": near_peer(i)},
            device_id_type=MESH,
        ).start()

    def others_of(buffer, count, sem):
        others = buffer.at[pl.ds(0, count - 1)]
        return pltpu.make_async_copy(others, others, sem)

    others_of(request, near, req_recv).wait()

    asked = jnp.concatenate(
        [jnp.broadcast_to(request[d], (2 * held, PIX)) for d in range(near)], axis=0
    )
    place = lax.rem(iota((near * 2 * held, PIX), 0), 2 * held)
    wanted = (asked >> 10) == me_near * held + (place >> 1)
    found = jnp.sum(jnp.where(wanted, (asked & 1023) + 1, 0), axis=1, keepdims=True)
    spot = jnp.where(found > 0, found - 1 + (place[:, 0:1] & 1) * 64, -1)
    select = jnp.where(iota((near * 2 * held, FAR * PIX), 1) == spot, 1.0, 0.0)
    select = select.astype(jnp.float32).astype(jnp.bfloat16)

    others_of(pixels, FAR, pix_recv).wait()
    blocks = jnp.dot(
        select, pixels[...].reshape(FAR * PIX, PIX), preferred_element_type=jnp.float32
    ).astype(jnp.bfloat16)
    packed[...] = blocks.reshape(near, 2 * held, PIX)

    for i in range(1, near):
        pltpu.make_async_remote_copy(
            src_ref=packed.at[near_index(i)],
            dst_ref=received.at[me_near],
            send_sem=data_send,
            recv_sem=data_recv,
            device_id={"brick": near_peer(i)},
            device_id_type=MESH,
        ).start()
    received[me_near] = packed[me_near]
    others_of(received, near, data_recv).wait()

    rowbuf[...] = jnp.dot(
        pick, received[...].reshape(near * 2 * held, PIX), preferred_element_type=jnp.float32
    )

    inner = groups * ROWS_DEV

    def place_slot(f, m, carry):
        s = f * MAXB + m
        offset = vox_ref[f, 0, m]
        target = jnp.where(offset == 0, inner, jnp.where(offset == inner + 1, inner + 1, offset - 1))
        target = jnp.where(m < count_ref[f], target, -1)
        hit = iota((inner + 8, PIX), 0) == target
        start = pl.multiple_of(s * PIX, PIX)
        parts = []
        for c in range(2):
            value = jnp.broadcast_to(rowbuf[pl.ds(c * SLOTS + s, 1), :], (inner + 8, PIX))
            parts.append(jnp.where(hit, value, 0.0))
        for g in range(groups):
            for c in range(2):
                lhs[pl.ds((2 * g + c) * ROWS_DEV, ROWS_DEV), pl.ds(start, PIX)] = parts[c][
                    g * ROWS_DEV : (g + 1) * ROWS_DEV
                ].astype(jnp.bfloat16)
        lhs[pl.ds(2 * inner, 16), pl.ds(start, PIX)] = jnp.concatenate(
            [part[inner:] for part in parts], axis=0
        ).astype(jnp.bfloat16)
        return carry

    def place_frame(f, carry):
        return lax.fori_loop(0, MAXB, functools.partial(place_slot, f), carry)

    lax.fori_loop(0, FR_DEV, place_frame, 0)
    for copy in splits:
        copy.wait()

    def over_copy(side, half, step, owner):
        return pltpu.make_async_remote_copy(
            src_ref=over_send.at[side, half],
            dst_ref=over_recv.at[half, me_f],
            send_sem=over_send_sem.at[side],
            recv_sem=over_sem,
            device_id={"frame": owner, "brick": brick_peer(step)},
            device_id_type=MESH,
        )

    parts = WIDTH // PIX
    for half in range(HALVES):
        columns = pl.ds(half * WIDTH, WIDTH)
        acc[half] = jnp.dot(lhs[...], split[:, columns], preferred_element_type=jnp.float32)

        for side in range(2):
            for c in range(2):
                for n in range(parts):
                    over_send[side, half, pl.ds(c * parts + n, 1), :] = acc[
                        half, pl.ds(2 * inner + c * 8 + side, 1), pl.ds(n * PIX, PIX)
                    ]

        @pl.when(me_b > 0)
        def _():
            over_copy(0, half, bricks - 1, groups - 1).start()

        @pl.when(me_b < bricks - 1)
        def _():
            over_copy(1, half, 1, 0).start()

        for i in range(1, groups):
            peer = frame_peer(i)
            pltpu.make_async_remote_copy(
                src_ref=acc.at[half, pl.ds(peer * 2 * ROWS_DEV, 2 * ROWS_DEV)],
                dst_ref=partial.at[half, me_f],
                send_sem=sum_send.at[half],
                recv_sem=sum_recv.at[half],
                device_id={"frame": peer},
                device_id_type=MESH,
            ).start()
        partial[half, me_f] = acc[
            half, pl.ds(pl.multiple_of(me_f * 2 * ROWS_DEV, 2 * ROWS_DEV), 2 * ROWS_DEV), :
        ]

    for half in range(HALVES):
        columns = pl.ds(half * WIDTH, WIDTH)
        others = partial.at[half, pl.ds(0, groups - 1)]
        pltpu.make_async_copy(others, others, sum_recv.at[half]).wait()
        value = partial[half, 0]
        for g in range(1, groups):
            value = value + partial[half, g]
        total[:, columns] = value

    def take_overhang(at):
        pltpu.make_async_copy(over_recv, over_recv, over_sem).wait()
        for half in range(HALVES):
            value = over_recv[half, 0]
            for g in range(1, groups):
                value = value + over_recv[half, g]
            for c in range(2):
                for n in range(parts):
                    where = (pl.ds(c * ROWS_DEV + at, 1), pl.ds(half * WIDTH + n * PIX, PIX))
                    total[where] = total[where] + value[c * parts + n : c * parts + n + 1]

    @pl.when((me_f == groups - 1) & (me_b < bricks - 1))
    def _():
        take_overhang(ROWS_DEV - 1)

    @pl.when((me_f == 0) & (me_b > 0))
    def _():
        take_overhang(0)

    others_of(pixels, FAR, pix_send).wait()
    others_of(request, near, req_send).wait()
    others_of(packed, near, data_send).wait()
    for half in range(HALVES):
        others = partial.at[half, pl.ds(0, groups - 1)]
        pltpu.make_async_copy(others, others, sum_send.at[half]).wait()

    def sent_over(side):
        pltpu.make_async_copy(over_send.at[side], over_send.at[side], over_send_sem.at[side]).wait()

    @pl.when(me_b > 0)
    def _():
        sent_over(0)

    @pl.when(me_b < bricks - 1)
    def _():
        sent_over(1)


def on_device(intensity, correction, splitting, block_count, pix_index, vox_offset):
    bricks = lax.axis_size("brick")
    groups = lax.axis_size("frame")
    near = bricks // FAR
    message = 2 * CAP * FAR
    rows = 2 * groups * ROWS_DEV + 16
    hbm = pl.BlockSpec(memory_space=pltpu.HBM)
    dma = pltpu.SemaphoreType.DMA
    total = pl.pallas_call(
        functools.partial(kernel, bricks, groups),
        out_shape=jax.ShapeDtypeStruct((2 * ROWS_DEV, VOX), jnp.float32),
        in_specs=[hbm] * 6,
        out_specs=pl.BlockSpec(memory_space=pltpu.VMEM),
        scratch_shapes=[
            pltpu.SMEM((FR_DEV, 1, MAXB), jnp.int32),
            pltpu.SMEM((FR_DEV, 1, MAXB), jnp.int32),
            pltpu.SMEM((FR_DEV,), jnp.int32),
            pltpu.VMEM((FR_DEV, PB_DEV, PIX), jnp.float32),
            pltpu.VMEM((FR_DEV, PB_DEV, PIX), jnp.float32),
            pltpu.VMEM((SLOTS * PIX, VOX), jnp.bfloat16),
            pltpu.VMEM((FAR, 2 * FR_DEV * PB_DEV, PIX), jnp.bfloat16),
            pltpu.VMEM((near, 1, PIX), jnp.int32),
            pltpu.VMEM((near, message, PIX), jnp.bfloat16),
            pltpu.VMEM((near, message, PIX), jnp.bfloat16),
            pltpu.VMEM((2 * SLOTS, PIX), jnp.float32),
            pltpu.VMEM((rows, SLOTS * PIX), jnp.bfloat16),
            pltpu.VMEM((HALVES, rows, WIDTH), jnp.float32),
            pltpu.VMEM((HALVES, groups, 2 * ROWS_DEV, WIDTH), jnp.float32),
            pltpu.VMEM((2, HALVES, 2 * WIDTH // PIX, PIX), jnp.float32),
            pltpu.VMEM((HALVES, groups, 2 * WIDTH // PIX, PIX), jnp.float32),
            dma((5,)),
            dma((CHUNKS,)),
            dma,
            dma,
            dma,
            dma,
            dma,
            dma,
            dma((HALVES,)),
            dma((HALVES,)),
            dma((2,)),
            dma,
        ],
        compiler_params=pltpu.CompilerParams(
            collective_id=0, has_side_effects=True, vmem_limit_bytes=32 * 1024 * 1024
        ),
    )(
        *[
            pltpu.with_memory_space_constraint(x, pltpu.HBM)
            for x in (
                pix_index,
                vox_offset,
                block_count.reshape(FR_DEV),
                intensity,
                correction,
                splitting.reshape(SLOTS * PIX, VOX),
            )
        ]
    )
    weight = total[ROWS_DEV:]
    merged = total[:ROWS_DEV] / jnp.maximum(weight, 1.0)
    return (merged[None], weight[None])


def solution(mesh):
    placed = (
        P("frame", "brick", None),
        P("frame", "brick", None),
        P("frame", "brick", None, None, None),
        P("frame", "brick"),
        P("frame", "brick", None),
        P("frame", "brick", None),
    )
    return jax.shard_map(
        on_device,
        mesh=mesh,
        in_specs=placed,
        out_specs=(P("brick", "frame", None), P("brick", "frame", None)),
        check_vma=False,
    )
```

```python
import functools

import jax
import jax.numpy as jnp
from jax import lax
from jax.experimental import pallas as pl
from jax.experimental.pallas import tpu as pltpu
from jax.sharding import PartitionSpec as P

MESH = pl.DeviceIdType.MESH
CAP = 4
FR_DEV = 4
MAXB = 8
PB_DEV = 16
ROWS_DEV = 16
SLOTS = FR_DEV * MAXB
PIX = 128
VOX = 512
HALVES = 2
WIDTH = VOX // HALVES
CHUNKS = 4
LEVELS = 32767.0
FAR = 4


def iota(shape, dim):
    return lax.broadcasted_iota(jnp.int32, shape, dim)


def kernel(
    bricks,
    groups,
    pix_hbm,
    vox_hbm,
    count_hbm,
    intensity_hbm,
    correction_hbm,
    split_hbm,
    total,
    pix_ref,
    vox_ref,
    count_ref,
    inten,
    corr,
    split,
    pixels,
    request,
    packed,
    received,
    rowbuf,
    lhs,
    acc,
    coded,
    partial,
    scale,
    scales,
    over_send,
    over_recv,
    load_sem,
    split_sem,
    pix_send,
    pix_recv,
    req_send,
    req_recv,
    data_send,
    data_recv,
    sum_send,
    sum_recv,
    scale_send,
    scale_recv,
    over_send_sem,
    over_sem,
):
    me_f = lax.axis_index("frame")
    me_b = lax.axis_index("brick")
    near = bricks // FAR
    me_y = me_b // (2 * FAR)
    me_c = lax.rem(me_b, 2)
    me_far = lax.rem(me_b // 2, FAR)
    me_near = me_y * 2 + me_c
    held = CAP * FAR
    barrier = pltpu.get_barrier_semaphore()

    def brick_peer(i):
        return lax.rem(me_b + i, bricks)

    def brick_of(at_near, at_far):
        return (at_near // 2 * FAR + at_far) * 2 + lax.rem(at_near, 2)

    def near_index(i):
        return lax.rem(me_near + i, near)

    def near_peer(i):
        return brick_of(near_index(i), me_far)

    def far_peer(i):
        return brick_of(me_near, lax.rem(me_far + i, FAR))

    def frame_peer(i):
        return lax.rem(me_f + i, groups)

    for i in range(1, FAR):
        pl.semaphore_signal(
            barrier, inc=1, device_id={"brick": far_peer(i)}, device_id_type=MESH
        )
    for i in range(1, near):
        pl.semaphore_signal(
            barrier, inc=1, device_id={"brick": near_peer(i)}, device_id_type=MESH
        )
    for i in range(1, groups):
        pl.semaphore_signal(
            barrier, inc=1, device_id={"frame": frame_peer(i)}, device_id_type=MESH
        )

    tables = [
        pltpu.make_async_copy(pix_hbm, pix_ref, load_sem.at[0]),
        pltpu.make_async_copy(vox_hbm, vox_ref, load_sem.at[1]),
        pltpu.make_async_copy(count_hbm, count_ref, load_sem.at[2]),
    ]
    loads = [
        pltpu.make_async_copy(intensity_hbm, inten, load_sem.at[3]),
        pltpu.make_async_copy(correction_hbm, corr, load_sem.at[4]),
    ]
    depth = SLOTS * PIX // CHUNKS
    splits = [
        pltpu.make_async_copy(
            split_hbm.at[pl.ds(k * depth, depth)],
            split.at[pl.ds(k * depth, depth)],
            split_sem.at[k],
        )
        for k in range(CHUNKS)
    ]
    for copy in tables + loads + splits:
        copy.start()
    for copy in tables:
        copy.wait()

    lane = iota((1, PIX), 1)
    row = jnp.full((1, PIX), -1, jnp.int32)
    for s in range(SLOTS):
        row = jnp.where(lane == s, pix_ref[s // MAXB, 0, s % MAXB], row)
    sub2, lane2 = iota((SLOTS, PIX), 0), iota((SLOTS, PIX), 1)
    column = jnp.sum(
        jnp.where(sub2 == lane2, jnp.broadcast_to(row, (SLOTS, PIX)), 0), axis=1, keepdims=True
    )
    near_row = (row // (2 * FAR * PB_DEV)) * 2 + ((row >> 4) & 1)
    near_col = (column // (2 * FAR * PB_DEV)) * 2 + ((column >> 4) & 1)
    same = (jnp.broadcast_to(near_row, (SLOTS, PIX)) == near_col).astype(jnp.int32)
    rank_row = jnp.sum(jnp.where(sub2 < lane2, same, 0), axis=0, keepdims=True)
    rank_col = jnp.sum(jnp.where(lane2 < sub2, same, 0), axis=1, keepdims=True)
    where_row = ((row >> 5) & (FAR - 1)) * 128 + (lane >> 3) * PB_DEV + (row & 15)
    code = (near_row * held + rank_row) * 1024 + where_row
    request[me_near] = jnp.where(lane < SLOTS, code, -1)
    key = near_col * held + rank_col
    wide = iota((SLOTS, near * 2 * held), 1)
    pick = jnp.concatenate(
        [jnp.where(wide == key * 2 + c, 1.0, 0.0).astype(jnp.float32) for c in range(2)],
        axis=0,
    ).astype(jnp.bfloat16)

    for copy in loads:
        copy.wait()
    pixels[me_far] = jnp.concatenate(
        [inten[...].reshape(FR_DEV * PB_DEV, PIX), corr[...].reshape(FR_DEV * PB_DEV, PIX)],
        axis=0,
    ).astype(jnp.bfloat16)

    pl.semaphore_wait(barrier, FAR - 1 + near - 1 + groups - 1)

    for i in range(1, FAR):
        pltpu.make_async_remote_copy(
            src_ref=pixels.at[me_far],
            dst_ref=pixels.at[me_far],
            send_sem=pix_send,
            recv_sem=pix_recv,
            device_id={"brick": far_peer(i)},
            device_id_type=MESH,
        ).start()
    for i in range(1, near):
        pltpu.make_async_remote_copy(
            src_ref=request.at[me_near],
            dst_ref=request.at[me_near],
            send_sem=req_send,
            recv_sem=req_recv,
            device_id={"brick": near_peer(i)},
            device_id_type=MESH,
        ).start()

    def others_of(buffer, count, sem):
        others = buffer.at[pl.ds(0, count - 1)]
        return pltpu.make_async_copy(others, others, sem)

    others_of(request, near, req_recv).wait()

    asked = jnp.concatenate(
        [jnp.broadcast_to(request[d], (2 * held, PIX)) for d in range(near)], axis=0
    )
    place = lax.rem(iota((near * 2 * held, PIX), 0), 2 * held)
    wanted = (asked >> 10) == me_near * held + (place >> 1)
    found = jnp.sum(jnp.where(wanted, (asked & 1023) + 1, 0), axis=1, keepdims=True)
    spot = jnp.where(found > 0, found - 1 + (place[:, 0:1] & 1) * 64, -1)
    select = jnp.where(iota((near * 2 * held, FAR * PIX), 1) == spot, 1.0, 0.0)
    select = select.astype(jnp.float32).astype(jnp.bfloat16)

    others_of(pixels, FAR, pix_recv).wait()
    blocks = jnp.dot(
        select, pixels[...].reshape(FAR * PIX, PIX), preferred_element_type=jnp.float32
    ).astype(jnp.bfloat16)
    packed[...] = blocks.reshape(near, 2 * held, PIX)

    for i in range(1, near):
        pltpu.make_async_remote_copy(
            src_ref=packed.at[near_index(i)],
            dst_ref=received.at[me_near],
            send_sem=data_send,
            recv_sem=data_recv,
            device_id={"brick": near_peer(i)},
            device_id_type=MESH,
        ).start()
    received[me_near] = packed[me_near]
    others_of(received, near, data_recv).wait()

    rowbuf[...] = jnp.dot(
        pick, received[...].reshape(near * 2 * held, PIX), preferred_element_type=jnp.float32
    )

    inner = groups * ROWS_DEV

    def place_slot(f, m, carry):
        s = f * MAXB + m
        offset = vox_ref[f, 0, m]
        target = jnp.where(offset == 0, inner, jnp.where(offset == inner + 1, inner + 1, offset - 1))
        target = jnp.where(m < count_ref[f], target, -1)
        hit = iota((inner + 8, PIX), 0) == target
        start = pl.multiple_of(s * PIX, PIX)
        parts = []
        for c in range(2):
            value = jnp.broadcast_to(rowbuf[pl.ds(c * SLOTS + s, 1), :], (inner + 8, PIX))
            parts.append(jnp.where(hit, value, 0.0))
        for g in range(groups):
            for c in range(2):
                lhs[pl.ds((2 * g + c) * ROWS_DEV, ROWS_DEV), pl.ds(start, PIX)] = parts[c][
                    g * ROWS_DEV : (g + 1) * ROWS_DEV
                ].astype(jnp.bfloat16)
        lhs[pl.ds(2 * inner, 16), pl.ds(start, PIX)] = jnp.concatenate(
            [part[inner:] for part in parts], axis=0
        ).astype(jnp.bfloat16)
        return carry

    def place_frame(f, carry):
        return lax.fori_loop(0, MAXB, functools.partial(place_slot, f), carry)

    lax.fori_loop(0, FR_DEV, place_frame, 0)
    for copy in splits:
        copy.wait()

    def over_copy(side, half, step, owner):
        return pltpu.make_async_remote_copy(
            src_ref=over_send.at[side, half],
            dst_ref=over_recv.at[half, me_f],
            send_sem=over_send_sem.at[side],
            recv_sem=over_sem,
            device_id={"frame": owner, "brick": brick_peer(step)},
            device_id_type=MESH,
        )

    parts = WIDTH // PIX
    for half in range(HALVES):
        columns = pl.ds(half * WIDTH, WIDTH)
        acc[half] = jnp.dot(lhs[...], split[:, columns], preferred_element_type=jnp.float32)

        for side in range(2):
            for c in range(2):
                for n in range(parts):
                    over_send[side, half, pl.ds(c * parts + n, 1), :] = acc[
                        half, pl.ds(2 * inner + c * 8 + side, 1), pl.ds(n * PIX, PIX)
                    ]

        @pl.when(me_b > 0)
        def _():
            over_copy(0, half, bricks - 1, groups - 1).start()

        @pl.when(me_b < bricks - 1)
        def _():
            over_copy(1, half, 1, 0).start()

        sums = acc[half, pl.ds(0, 2 * inner), :].reshape(2 * groups, ROWS_DEV, WIDTH)
        top = jnp.max(jnp.abs(sums), axis=1, keepdims=True)
        unit = jnp.where(top > 0.0, LEVELS / jnp.maximum(top, 1e-33), 0.0)
        code = jnp.round(sums * unit).astype(jnp.int32).astype(jnp.int16)
        coded[half] = code.reshape(2 * inner, WIDTH)
        top = top * (1.0 / LEVELS)
        for g in range(groups):
            for c in range(2):
                for n in range(parts):
                    scale[half, g, pl.ds(c * parts + n, 1), :] = top[
                        2 * g + c, :, n * PIX : (n + 1) * PIX
                    ]

        for i in range(1, groups):
            peer = frame_peer(i)
            pltpu.make_async_remote_copy(
                src_ref=scale.at[half, peer],
                dst_ref=scales.at[half, me_f],
                send_sem=scale_send.at[half],
                recv_sem=scale_recv.at[half],
                device_id={"frame": peer},
                device_id_type=MESH,
            ).start()
            pltpu.make_async_remote_copy(
                src_ref=coded.at[half, pl.ds(peer * 2 * ROWS_DEV, 2 * ROWS_DEV)],
                dst_ref=partial.at[half, me_f],
                send_sem=sum_send.at[half],
                recv_sem=sum_recv.at[half],
                device_id={"frame": peer},
                device_id_type=MESH,
            ).start()
        partial[half, me_f] = jnp.zeros((2 * ROWS_DEV, WIDTH), jnp.int16)
        scales[half, me_f] = jnp.zeros((2 * parts, PIX), jnp.float32)
        total[:, columns] = acc[
            half, pl.ds(pl.multiple_of(me_f * 2 * ROWS_DEV, 2 * ROWS_DEV), 2 * ROWS_DEV), :
        ]

    for half in range(HALVES):
        others = partial.at[half, pl.ds(0, groups - 1)]
        pltpu.make_async_copy(others, others, sum_recv.at[half]).wait()
        others = scales.at[half, pl.ds(0, groups - 1)]
        pltpu.make_async_copy(others, others, scale_recv.at[half]).wait()
        for c in range(2):
            for n in range(parts):
                where = (pl.ds(c * ROWS_DEV, ROWS_DEV), pl.ds(half * WIDTH + n * PIX, PIX))
                value = total[where]
                for g in range(groups):
                    term = partial[
                        half, g, pl.ds(c * ROWS_DEV, ROWS_DEV), pl.ds(n * PIX, PIX)
                    ]
                    value = value + term.astype(jnp.float32) * scales[half, g, pl.ds(c * parts + n, 1), :]
                total[where] = value

    def take_overhang(at):
        pltpu.make_async_copy(over_recv, over_recv, over_sem).wait()
        for half in range(HALVES):
            value = over_recv[half, 0]
            for g in range(1, groups):
                value = value + over_recv[half, g]
            for c in range(2):
                for n in range(parts):
                    where = (pl.ds(c * ROWS_DEV + at, 1), pl.ds(half * WIDTH + n * PIX, PIX))
                    total[where] = total[where] + value[c * parts + n : c * parts + n + 1]

    @pl.when((me_f == groups - 1) & (me_b < bricks - 1))
    def _():
        take_overhang(ROWS_DEV - 1)

    @pl.when((me_f == 0) & (me_b > 0))
    def _():
        take_overhang(0)

    others_of(pixels, FAR, pix_send).wait()
    others_of(request, near, req_send).wait()
    others_of(packed, near, data_send).wait()
    for half in range(HALVES):
        others = partial.at[half, pl.ds(0, groups - 1)]
        pltpu.make_async_copy(others, others, sum_send.at[half]).wait()
        others = scales.at[half, pl.ds(0, groups - 1)]
        pltpu.make_async_copy(others, others, scale_send.at[half]).wait()

    def sent_over(side):
        pltpu.make_async_copy(over_send.at[side], over_send.at[side], over_send_sem.at[side]).wait()

    @pl.when(me_b > 0)
    def _():
        sent_over(0)

    @pl.when(me_b < bricks - 1)
    def _():
        sent_over(1)


def on_device(intensity, correction, splitting, block_count, pix_index, vox_offset):
    bricks = lax.axis_size("brick")
    groups = lax.axis_size("frame")
    near = bricks // FAR
    message = 2 * CAP * FAR
    rows = 2 * groups * ROWS_DEV + 16
    hbm = pl.BlockSpec(memory_space=pltpu.HBM)
    dma = pltpu.SemaphoreType.DMA
    total = pl.pallas_call(
        functools.partial(kernel, bricks, groups),
        out_shape=jax.ShapeDtypeStruct((2 * ROWS_DEV, VOX), jnp.float32),
        in_specs=[hbm] * 6,
        out_specs=pl.BlockSpec(memory_space=pltpu.VMEM),
        scratch_shapes=[
            pltpu.SMEM((FR_DEV, 1, MAXB), jnp.int32),
            pltpu.SMEM((FR_DEV, 1, MAXB), jnp.int32),
            pltpu.SMEM((FR_DEV,), jnp.int32),
            pltpu.VMEM((FR_DEV, PB_DEV, PIX), jnp.float32),
            pltpu.VMEM((FR_DEV, PB_DEV, PIX), jnp.float32),
            pltpu.VMEM((SLOTS * PIX, VOX), jnp.bfloat16),
            pltpu.VMEM((FAR, 2 * FR_DEV * PB_DEV, PIX), jnp.bfloat16),
            pltpu.VMEM((near, 1, PIX), jnp.int32),
            pltpu.VMEM((near, message, PIX), jnp.bfloat16),
            pltpu.VMEM((near, message, PIX), jnp.bfloat16),
            pltpu.VMEM((2 * SLOTS, PIX), jnp.float32),
            pltpu.VMEM((rows, SLOTS * PIX), jnp.bfloat16),
            pltpu.VMEM((HALVES, rows, WIDTH), jnp.float32),
            pltpu.VMEM((HALVES, 2 * groups * ROWS_DEV, WIDTH), jnp.int16),
            pltpu.VMEM((HALVES, groups, 2 * ROWS_DEV, WIDTH), jnp.int16),
            pltpu.VMEM((HALVES, groups, 2 * WIDTH // PIX, PIX), jnp.float32),
            pltpu.VMEM((HALVES, groups, 2 * WIDTH // PIX, PIX), jnp.float32),
            pltpu.VMEM((2, HALVES, 2 * WIDTH // PIX, PIX), jnp.float32),
            pltpu.VMEM((HALVES, groups, 2 * WIDTH // PIX, PIX), jnp.float32),
            dma((5,)),
            dma((CHUNKS,)),
            dma,
            dma,
            dma,
            dma,
            dma,
            dma,
            dma((HALVES,)),
            dma((HALVES,)),
            dma((HALVES,)),
            dma((HALVES,)),
            dma((2,)),
            dma,
        ],
        compiler_params=pltpu.CompilerParams(
            collective_id=0, has_side_effects=True, vmem_limit_bytes=32 * 1024 * 1024
        ),
    )(
        *[
            pltpu.with_memory_space_constraint(x, pltpu.HBM)
            for x in (
                pix_index,
                vox_offset,
                block_count.reshape(FR_DEV),
                intensity,
                correction,
                splitting.reshape(SLOTS * PIX, VOX),
            )
        ]
    )
    weight = total[ROWS_DEV:]
    merged = total[:ROWS_DEV] / jnp.maximum(weight, 1.0)
    return (merged[None], weight[None])


def solution(mesh):
    placed = (
        P("frame", "brick", None),
        P("frame", "brick", None),
        P("frame", "brick", None, None, None),
        P("frame", "brick"),
        P("frame", "brick", None),
        P("frame", "brick", None),
    )
    return jax.shard_map(
        on_device,
        mesh=mesh,
        in_specs=placed,
        out_specs=(P("brick", "frame", None), P("brick", "frame", None)),
        check_vma=False,
    )
```

```python
import functools

import jax
import jax.numpy as jnp
from jax import lax
from jax.experimental import pallas as pl
from jax.experimental.pallas import tpu as pltpu
from jax.sharding import PartitionSpec as P

MESH = pl.DeviceIdType.MESH
CAP = 4
FR_DEV = 4
MAXB = 8
PB_DEV = 16
ROWS_DEV = 16
SLOTS = FR_DEV * MAXB
PIX = 128
VOX = 512
HALVES = 2
WIDTH = VOX // HALVES
CHUNKS = 4
LEVELS = 32767.0
FAR = 4


def iota(shape, dim):
    return lax.broadcasted_iota(jnp.int32, shape, dim)


def kernel(
    bricks,
    groups,
    pix_hbm,
    vox_hbm,
    count_hbm,
    intensity_hbm,
    correction_hbm,
    split_hbm,
    total,
    pix_ref,
    vox_ref,
    count_ref,
    inten,
    corr,
    split,
    pixels,
    request,
    packed,
    received,
    lhs,
    placer,
    acc,
    coded,
    partial,
    scale,
    scales,
    over_send,
    over_recv,
    load_sem,
    split_sem,
    pix_send,
    pix_recv,
    req_send,
    req_recv,
    data_send,
    data_recv,
    sum_send,
    sum_recv,
    scale_send,
    scale_recv,
    over_send_sem,
    over_sem,
):
    me_f = lax.axis_index("frame")
    me_b = lax.axis_index("brick")
    near = bricks // FAR
    me_far = me_b // near
    me_near = lax.rem(me_b, near)
    held = CAP * FAR
    barrier = pltpu.get_barrier_semaphore()

    def brick_peer(i):
        return lax.rem(me_b + i, bricks)

    def brick_of(at_near, at_far):
        return at_far * near + at_near

    order = sorted(range(1, near), key=lambda i: (-min(i, near - i), i))

    def near_index(i):
        return lax.rem(me_near + i, near)

    def near_peer(i):
        return brick_of(near_index(i), me_far)

    def far_peer(i):
        return brick_of(me_near, lax.rem(me_far + i, FAR))

    def frame_peer(i):
        return lax.rem(me_f + i, groups)

    for i in order:
        pl.semaphore_signal(
            barrier, inc=1, device_id={"brick": near_peer(i)}, device_id_type=MESH
        )
    for i in range(1, FAR):
        pl.semaphore_signal(
            barrier, inc=1, device_id={"brick": far_peer(i)}, device_id_type=MESH
        )
    for i in range(1, groups):
        pl.semaphore_signal(
            barrier, inc=1, device_id={"frame": frame_peer(i)}, device_id_type=MESH
        )

    tables = [
        pltpu.make_async_copy(pix_hbm, pix_ref, load_sem.at[0]),
        pltpu.make_async_copy(vox_hbm, vox_ref, load_sem.at[1]),
        pltpu.make_async_copy(count_hbm, count_ref, load_sem.at[2]),
    ]
    loads = [
        pltpu.make_async_copy(intensity_hbm, inten, load_sem.at[3]),
        pltpu.make_async_copy(correction_hbm, corr, load_sem.at[4]),
    ]
    depth = SLOTS * PIX // CHUNKS
    splits = [
        pltpu.make_async_copy(
            split_hbm.at[pl.ds(k * depth, depth)],
            split.at[pl.ds(k * depth, depth)],
            split_sem.at[k],
        )
        for k in range(CHUNKS)
    ]
    for copy in tables + loads + splits:
        copy.start()
    for copy in tables:
        copy.wait()

    lane = iota((1, PIX), 1)
    row = jnp.full((1, PIX), -1, jnp.int32)
    for s in range(SLOTS):
        row = jnp.where(lane == s, pix_ref[s // MAXB, 0, s % MAXB], row)
    sub2, lane2 = iota((SLOTS, PIX), 0), iota((SLOTS, PIX), 1)
    column = jnp.sum(
        jnp.where(sub2 == lane2, jnp.broadcast_to(row, (SLOTS, PIX)), 0), axis=1, keepdims=True
    )
    near_row = (row >> 4) & (near - 1)
    near_col = (column >> 4) & (near - 1)
    same = (jnp.broadcast_to(near_row, (SLOTS, PIX)) == near_col).astype(jnp.int32)
    rank_row = jnp.sum(jnp.where(sub2 < lane2, same, 0), axis=0, keepdims=True)
    rank_col = jnp.sum(jnp.where(lane2 < sub2, same, 0), axis=1, keepdims=True)
    where_row = (row // (near * PB_DEV)) * 128 + (lane >> 3) * PB_DEV + (row & 15)
    code = (near_row * held + rank_row) * 1024 + where_row
    request[me_near] = jnp.where(lane < SLOTS, code, -1)
    key = near_col * held + rank_col
    wide = iota((SLOTS, near * 2 * held), 1)
    pick = jnp.concatenate(
        [jnp.where(wide == key * 2 + c, 1.0, 0.0).astype(jnp.float32) for c in range(2)],
        axis=0,
    ).astype(jnp.bfloat16)

    inner = groups * ROWS_DEV
    rows = 2 * inner + 16
    pieces = 3
    wide_lane = iota((1, pieces * 2 * SLOTS), 1)
    voxel = jnp.full((1, pieces * 2 * SLOTS), -1, jnp.int32)
    for s in range(SLOTS):
        f, m = s // MAXB, s % MAXB
        offset = vox_ref[f, 0, m]
        target = jnp.where(offset == 0, inner, jnp.where(offset == inner + 1, inner + 1, offset - 1))
        target = jnp.where(m < count_ref[f], target, -1)
        voxel = jnp.where((wide_lane & (SLOTS - 1)) == s, target, voxel)
    down = iota((rows, pieces * 2 * SLOTS), 0)
    tail = down >= 2 * inner
    own_voxel = jnp.where(tail, inner + (down & 7), (down >> 5) * ROWS_DEV + (down & 15))
    own_channel = jnp.where(tail, (down >> 3) & 1, (down >> 4) & 1)
    channel = (iota((rows, pieces * 2 * SLOTS), 1) // SLOTS) & 1
    hit = (own_voxel == voxel) & (own_channel == channel)
    placer[...] = jnp.where(hit, 1.0, 0.0).astype(jnp.float32).astype(jnp.bfloat16)

    for copy in loads:
        copy.wait()
    pixels[me_far] = jnp.concatenate(
        [inten[...].reshape(FR_DEV * PB_DEV, PIX), corr[...].reshape(FR_DEV * PB_DEV, PIX)],
        axis=0,
    ).astype(jnp.bfloat16)

    pl.semaphore_wait(barrier, FAR - 1 + near - 1 + groups - 1)

    for i in order:
        pltpu.make_async_remote_copy(
            src_ref=request.at[me_near],
            dst_ref=request.at[me_near],
            send_sem=req_send,
            recv_sem=req_recv,
            device_id={"brick": near_peer(i)},
            device_id_type=MESH,
        ).start()
    for i in range(1, FAR):
        pltpu.make_async_remote_copy(
            src_ref=pixels.at[me_far],
            dst_ref=pixels.at[me_far],
            send_sem=pix_send,
            recv_sem=pix_recv,
            device_id={"brick": far_peer(i)},
            device_id_type=MESH,
        ).start()

    def others_of(buffer, count, sem):
        others = buffer.at[pl.ds(0, count - 1)]
        return pltpu.make_async_copy(others, others, sem)

    others_of(request, near, req_recv).wait()

    asked = jnp.concatenate(
        [jnp.broadcast_to(request[d], (2 * held, PIX)) for d in range(near)], axis=0
    )
    place = lax.rem(iota((near * 2 * held, PIX), 0), 2 * held)
    wanted = (asked >> 10) == me_near * held + (place >> 1)
    found = jnp.sum(jnp.where(wanted, (asked & 1023) + 1, 0), axis=1, keepdims=True)
    spot = jnp.where(found > 0, found - 1 + (place[:, 0:1] & 1) * 64, -1)
    select = jnp.where(iota((near * 2 * held, FAR * PIX), 1) == spot, 1.0, 0.0)
    select = select.astype(jnp.float32).astype(jnp.bfloat16)

    others_of(pixels, FAR, pix_recv).wait()
    blocks = jnp.dot(
        select, pixels[...].reshape(FAR * PIX, PIX), preferred_element_type=jnp.float32
    ).astype(jnp.bfloat16)
    packed[...] = blocks.reshape(near, 2 * held, PIX)

    for i in order:
        pltpu.make_async_remote_copy(
            src_ref=packed.at[near_index(i)],
            dst_ref=received.at[me_near],
            send_sem=data_send,
            recv_sem=data_recv,
            device_id={"brick": near_peer(i)},
            device_id_type=MESH,
        ).start()
    received[me_near] = packed[me_near]
    others_of(received, near, data_recv).wait()

    rows_of = jnp.dot(
        pick, received[...].reshape(near * 2 * held, PIX), preferred_element_type=jnp.float32
    )
    slot = iota((2 * SLOTS, PIX), 0) & (SLOTS - 1)
    for s in range(SLOTS):
        lhs[:, s * PIX : (s + 1) * PIX] = jnp.where(slot == s, rows_of, 0.0).astype(jnp.bfloat16)
    for copy in splits:
        copy.wait()

    def over_copy(side, half, step, owner):
        return pltpu.make_async_remote_copy(
            src_ref=over_send.at[side, half],
            dst_ref=over_recv.at[half, me_f],
            send_sem=over_send_sem.at[side],
            recv_sem=over_sem,
            device_id={"frame": owner, "brick": brick_peer(step)},
            device_id_type=MESH,
        )

    parts = WIDTH // PIX
    for half in range(HALVES):
        columns = pl.ds(half * WIDTH, WIDTH)
        contrib = jnp.dot(lhs[...], split[:, columns], preferred_element_type=jnp.float32)
        first = contrib.astype(jnp.bfloat16)
        left = contrib - first.astype(jnp.float32)
        second = left.astype(jnp.bfloat16)
        third = (left - second.astype(jnp.float32)).astype(jnp.bfloat16)
        acc[half] = jnp.dot(
            placer[...],
            jnp.concatenate([first, second, third], axis=0),
            preferred_element_type=jnp.float32,
        )

        for side in range(2):
            for c in range(2):
                for n in range(parts):
                    over_send[side, half, pl.ds(c * parts + n, 1), :] = acc[
                        half, pl.ds(2 * inner + c * 8 + side, 1), pl.ds(n * PIX, PIX)
                    ]

        @pl.when(me_b > 0)
        def _():
            over_copy(0, half, bricks - 1, groups - 1).start()

        @pl.when(me_b < bricks - 1)
        def _():
            over_copy(1, half, 1, 0).start()

        sums = acc[half, pl.ds(0, 2 * inner), :].reshape(2 * groups, ROWS_DEV, WIDTH)
        top = jnp.max(jnp.abs(sums), axis=1, keepdims=True)
        unit = jnp.where(top > 0.0, LEVELS / jnp.maximum(top, 1e-33), 0.0)
        code = jnp.round(sums * unit).astype(jnp.int32).astype(jnp.int16)
        coded[half] = code.reshape(2 * inner, WIDTH)
        top = top * (1.0 / LEVELS)
        for g in range(groups):
            for c in range(2):
                for n in range(parts):
                    scale[half, g, pl.ds(c * parts + n, 1), :] = top[
                        2 * g + c, :, n * PIX : (n + 1) * PIX
                    ]

        for i in range(1, groups):
            peer = frame_peer(i)
            pltpu.make_async_remote_copy(
                src_ref=scale.at[half, peer],
                dst_ref=scales.at[half, me_f],
                send_sem=scale_send.at[half],
                recv_sem=scale_recv.at[half],
                device_id={"frame": peer},
                device_id_type=MESH,
            ).start()
            pltpu.make_async_remote_copy(
                src_ref=coded.at[half, pl.ds(peer * 2 * ROWS_DEV, 2 * ROWS_DEV)],
                dst_ref=partial.at[half, me_f],
                send_sem=sum_send.at[half],
                recv_sem=sum_recv.at[half],
                device_id={"frame": peer},
                device_id_type=MESH,
            ).start()
        partial[half, me_f] = jnp.zeros((2 * ROWS_DEV, WIDTH), jnp.int16)
        scales[half, me_f] = jnp.zeros((2 * parts, PIX), jnp.float32)
        total[:, columns] = acc[
            half, pl.ds(pl.multiple_of(me_f * 2 * ROWS_DEV, 2 * ROWS_DEV), 2 * ROWS_DEV), :
        ]

    for half in range(HALVES):
        others = partial.at[half, pl.ds(0, groups - 1)]
        pltpu.make_async_copy(others, others, sum_recv.at[half]).wait()
        others = scales.at[half, pl.ds(0, groups - 1)]
        pltpu.make_async_copy(others, others, scale_recv.at[half]).wait()
        for c in range(2):
            for n in range(parts):
                where = (pl.ds(c * ROWS_DEV, ROWS_DEV), pl.ds(half * WIDTH + n * PIX, PIX))
                value = total[where]
                for g in range(groups):
                    term = partial[
                        half, g, pl.ds(c * ROWS_DEV, ROWS_DEV), pl.ds(n * PIX, PIX)
                    ]
                    value = value + term.astype(jnp.float32) * scales[half, g, pl.ds(c * parts + n, 1), :]
                total[where] = value

    def take_overhang(at):
        pltpu.make_async_copy(over_recv, over_recv, over_sem).wait()
        for half in range(HALVES):
            value = over_recv[half, 0]
            for g in range(1, groups):
                value = value + over_recv[half, g]
            for c in range(2):
                for n in range(parts):
                    where = (pl.ds(c * ROWS_DEV + at, 1), pl.ds(half * WIDTH + n * PIX, PIX))
                    total[where] = total[where] + value[c * parts + n : c * parts + n + 1]

    @pl.when((me_f == groups - 1) & (me_b < bricks - 1))
    def _():
        take_overhang(ROWS_DEV - 1)

    @pl.when((me_f == 0) & (me_b > 0))
    def _():
        take_overhang(0)

    others_of(pixels, FAR, pix_send).wait()
    others_of(request, near, req_send).wait()
    others_of(packed, near, data_send).wait()
    for half in range(HALVES):
        others = partial.at[half, pl.ds(0, groups - 1)]
        pltpu.make_async_copy(others, others, sum_send.at[half]).wait()
        others = scales.at[half, pl.ds(0, groups - 1)]
        pltpu.make_async_copy(others, others, scale_send.at[half]).wait()

    def sent_over(side):
        pltpu.make_async_copy(over_send.at[side], over_send.at[side], over_send_sem.at[side]).wait()

    @pl.when(me_b > 0)
    def _():
        sent_over(0)

    @pl.when(me_b < bricks - 1)
    def _():
        sent_over(1)


def on_device(intensity, correction, splitting, block_count, pix_index, vox_offset):
    bricks = lax.axis_size("brick")
    groups = lax.axis_size("frame")
    near = bricks // FAR
    message = 2 * CAP * FAR
    rows = 2 * groups * ROWS_DEV + 16
    hbm = pl.BlockSpec(memory_space=pltpu.HBM)
    dma = pltpu.SemaphoreType.DMA
    total = pl.pallas_call(
        functools.partial(kernel, bricks, groups),
        out_shape=jax.ShapeDtypeStruct((2 * ROWS_DEV, VOX), jnp.float32),
        in_specs=[hbm] * 6,
        out_specs=pl.BlockSpec(memory_space=pltpu.VMEM),
        scratch_shapes=[
            pltpu.SMEM((FR_DEV, 1, MAXB), jnp.int32),
            pltpu.SMEM((FR_DEV, 1, MAXB), jnp.int32),
            pltpu.SMEM((FR_DEV,), jnp.int32),
            pltpu.VMEM((FR_DEV, PB_DEV, PIX), jnp.float32),
            pltpu.VMEM((FR_DEV, PB_DEV, PIX), jnp.float32),
            pltpu.VMEM((SLOTS * PIX, VOX), jnp.bfloat16),
            pltpu.VMEM((FAR, 2 * FR_DEV * PB_DEV, PIX), jnp.bfloat16),
            pltpu.VMEM((near, 1, PIX), jnp.int32),
            pltpu.VMEM((near, message, PIX), jnp.bfloat16),
            pltpu.VMEM((near, message, PIX), jnp.bfloat16),
            pltpu.VMEM((2 * SLOTS, SLOTS * PIX), jnp.bfloat16),
            pltpu.VMEM((rows, 6 * SLOTS), jnp.bfloat16),
            pltpu.VMEM((HALVES, rows, WIDTH), jnp.float32),
            pltpu.VMEM((HALVES, 2 * groups * ROWS_DEV, WIDTH), jnp.int16),
            pltpu.VMEM((HALVES, groups, 2 * ROWS_DEV, WIDTH), jnp.int16),
            pltpu.VMEM((HALVES, groups, 2 * WIDTH // PIX, PIX), jnp.float32),
            pltpu.VMEM((HALVES, groups, 2 * WIDTH // PIX, PIX), jnp.float32),
            pltpu.VMEM((2, HALVES, 2 * WIDTH // PIX, PIX), jnp.float32),
            pltpu.VMEM((HALVES, groups, 2 * WIDTH // PIX, PIX), jnp.float32),
            dma((5,)),
            dma((CHUNKS,)),
            dma,
            dma,
            dma,
            dma,
            dma,
            dma,
            dma((HALVES,)),
            dma((HALVES,)),
            dma((HALVES,)),
            dma((HALVES,)),
            dma((2,)),
            dma,
        ],
        compiler_params=pltpu.CompilerParams(
            collective_id=0, has_side_effects=True, vmem_limit_bytes=32 * 1024 * 1024
        ),
    )(
        *[
            pltpu.with_memory_space_constraint(x, pltpu.HBM)
            for x in (
                pix_index,
                vox_offset,
                block_count.reshape(FR_DEV),
                intensity,
                correction,
                splitting.reshape(SLOTS * PIX, VOX),
            )
        ]
    )
    weight = total[ROWS_DEV:]
    merged = total[:ROWS_DEV] / jnp.maximum(weight, 1.0)
    return (merged[None], weight[None])


def solution(mesh):
    placed = (
        P("frame", "brick", None),
        P("frame", "brick", None),
        P("frame", "brick", None, None, None),
        P("frame", "brick"),
        P("frame", "brick", None),
        P("frame", "brick", None),
    )
    return jax.shard_map(
        on_device,
        mesh=mesh,
        in_specs=placed,
        out_specs=(P("brick", "frame", None), P("brick", "frame", None)),
        check_vma=False,
    )
```

```python
import functools

import jax
import jax.numpy as jnp
from jax import lax
from jax.experimental import pallas as pl
from jax.experimental.pallas import tpu as pltpu
from jax.sharding import PartitionSpec as P

MESH = pl.DeviceIdType.MESH
CAP = 4
FR_DEV = 4
MAXB = 8
PB_DEV = 16
ROWS_DEV = 16
SLOTS = FR_DEV * MAXB
PIX = 128
VOX = 512
HALVES = 1
WIDTH = VOX // HALVES
CHUNKS = 4
LEVELS = 32767.0
FAR = 4


def iota(shape, dim):
    return lax.broadcasted_iota(jnp.int32, shape, dim)


def kernel(
    bricks,
    groups,
    pix_hbm,
    vox_hbm,
    count_hbm,
    intensity_hbm,
    correction_hbm,
    split_hbm,
    total,
    pix_ref,
    vox_ref,
    count_ref,
    inten,
    corr,
    split,
    pixels,
    request,
    packed,
    received,
    lhs,
    placer,
    acc,
    coded,
    partial,
    scale,
    scales,
    over_send,
    over_recv,
    load_sem,
    split_sem,
    pix_send,
    pix_recv,
    req_send,
    req_recv,
    data_send,
    data_recv,
    sum_send,
    sum_recv,
    scale_send,
    scale_recv,
    over_send_sem,
    over_sem,
):
    me_f = lax.axis_index("frame")
    me_b = lax.axis_index("brick")
    near = bricks // FAR
    me_far = me_b // near
    me_near = lax.rem(me_b, near)
    held = CAP * FAR
    barrier = pltpu.get_barrier_semaphore()

    def brick_peer(i):
        return lax.rem(me_b + i, bricks)

    def brick_of(at_near, at_far):
        return at_far * near + at_near

    order = sorted(range(1, near), key=lambda i: (-min(i, near - i), i))

    def near_index(i):
        return lax.rem(me_near + i, near)

    def near_peer(i):
        return brick_of(near_index(i), me_far)

    def far_peer(i):
        return brick_of(me_near, lax.rem(me_far + i, FAR))

    def frame_peer(i):
        return lax.rem(me_f + i, groups)

    for i in order:
        pl.semaphore_signal(
            barrier, inc=1, device_id={"brick": near_peer(i)}, device_id_type=MESH
        )
    for i in range(1, FAR):
        pl.semaphore_signal(
            barrier, inc=1, device_id={"brick": far_peer(i)}, device_id_type=MESH
        )
    for i in range(1, groups):
        pl.semaphore_signal(
            barrier, inc=1, device_id={"frame": frame_peer(i)}, device_id_type=MESH
        )

    tables = [
        pltpu.make_async_copy(pix_hbm, pix_ref, load_sem.at[0]),
        pltpu.make_async_copy(vox_hbm, vox_ref, load_sem.at[1]),
        pltpu.make_async_copy(count_hbm, count_ref, load_sem.at[2]),
    ]
    loads = [
        pltpu.make_async_copy(intensity_hbm, inten, load_sem.at[3]),
        pltpu.make_async_copy(correction_hbm, corr, load_sem.at[4]),
    ]
    depth = SLOTS * PIX // CHUNKS
    splits = [
        pltpu.make_async_copy(
            split_hbm.at[pl.ds(k * depth, depth)],
            split.at[pl.ds(k * depth, depth)],
            split_sem.at[k],
        )
        for k in range(CHUNKS)
    ]
    for copy in tables + loads + splits:
        copy.start()
    for copy in tables:
        copy.wait()

    lane = iota((1, PIX), 1)
    row = jnp.full((1, PIX), -1, jnp.int32)
    for s in range(SLOTS):
        row = jnp.where(lane == s, pix_ref[s // MAXB, 0, s % MAXB], row)
    sub2, lane2 = iota((SLOTS, PIX), 0), iota((SLOTS, PIX), 1)
    column = jnp.sum(
        jnp.where(sub2 == lane2, jnp.broadcast_to(row, (SLOTS, PIX)), 0), axis=1, keepdims=True
    )
    near_row = (row >> 4) & (near - 1)
    near_col = (column >> 4) & (near - 1)
    same = (jnp.broadcast_to(near_row, (SLOTS, PIX)) == near_col).astype(jnp.int32)
    rank_row = jnp.sum(jnp.where(sub2 < lane2, same, 0), axis=0, keepdims=True)
    rank_col = jnp.sum(jnp.where(lane2 < sub2, same, 0), axis=1, keepdims=True)
    where_row = (row // (near * PB_DEV)) * 128 + (lane >> 3) * PB_DEV + (row & 15)
    code = (near_row * held + rank_row) * 1024 + where_row
    request[me_near] = jnp.where(lane < SLOTS, code, -1)
    key = near_col * held + rank_col
    wide = iota((SLOTS, near * 2 * held), 1)
    pick = jnp.concatenate(
        [jnp.where(wide == key * 2 + c, 1.0, 0.0).astype(jnp.float32) for c in range(2)],
        axis=0,
    ).astype(jnp.bfloat16)

    inner = groups * ROWS_DEV
    rows = 2 * inner + 16
    pieces = 3
    wide_lane = iota((1, pieces * 2 * SLOTS), 1)
    voxel = jnp.full((1, pieces * 2 * SLOTS), -1, jnp.int32)
    for s in range(SLOTS):
        f, m = s // MAXB, s % MAXB
        offset = vox_ref[f, 0, m]
        target = jnp.where(offset == 0, inner, jnp.where(offset == inner + 1, inner + 1, offset - 1))
        target = jnp.where(m < count_ref[f], target, -1)
        voxel = jnp.where((wide_lane & (SLOTS - 1)) == s, target, voxel)
    down = iota((rows, pieces * 2 * SLOTS), 0)
    tail = down >= 2 * inner
    own_voxel = jnp.where(tail, inner + (down & 7), (down >> 5) * ROWS_DEV + (down & 15))
    own_channel = jnp.where(tail, (down >> 3) & 1, (down >> 4) & 1)
    channel = (iota((rows, pieces * 2 * SLOTS), 1) // SLOTS) & 1
    hit = (own_voxel == voxel) & (own_channel == channel)
    placer[...] = jnp.where(hit, 1.0, 0.0).astype(jnp.float32).astype(jnp.bfloat16)

    for copy in loads:
        copy.wait()
    pixels[me_far] = jnp.concatenate(
        [inten[...].reshape(FR_DEV * PB_DEV, PIX), corr[...].reshape(FR_DEV * PB_DEV, PIX)],
        axis=0,
    ).astype(jnp.bfloat16)

    pl.semaphore_wait(barrier, FAR - 1 + near - 1 + groups - 1)

    for i in order:
        pltpu.make_async_remote_copy(
            src_ref=request.at[me_near],
            dst_ref=request.at[me_near],
            send_sem=req_send,
            recv_sem=req_recv,
            device_id={"brick": near_peer(i)},
            device_id_type=MESH,
        ).start()
    for i in range(1, FAR):
        pltpu.make_async_remote_copy(
            src_ref=pixels.at[me_far],
            dst_ref=pixels.at[me_far],
            send_sem=pix_send,
            recv_sem=pix_recv,
            device_id={"brick": far_peer(i)},
            device_id_type=MESH,
        ).start()

    def others_of(buffer, count, sem):
        others = buffer.at[pl.ds(0, count - 1)]
        return pltpu.make_async_copy(others, others, sem)

    others_of(request, near, req_recv).wait()

    asked = jnp.concatenate(
        [jnp.broadcast_to(request[d], (2 * held, PIX)) for d in range(near)], axis=0
    )
    place = lax.rem(iota((near * 2 * held, PIX), 0), 2 * held)
    wanted = (asked >> 10) == me_near * held + (place >> 1)
    found = jnp.sum(jnp.where(wanted, (asked & 1023) + 1, 0), axis=1, keepdims=True)
    spot = jnp.where(found > 0, found - 1 + (place[:, 0:1] & 1) * 64, -1)
    select = jnp.where(iota((near * 2 * held, FAR * PIX), 1) == spot, 1.0, 0.0)
    select = select.astype(jnp.float32).astype(jnp.bfloat16)

    others_of(pixels, FAR, pix_recv).wait()
    blocks = jnp.dot(
        select, pixels[...].reshape(FAR * PIX, PIX), preferred_element_type=jnp.float32
    ).astype(jnp.bfloat16)
    packed[...] = blocks.reshape(near, 2 * held, PIX)

    for i in order:
        pltpu.make_async_remote_copy(
            src_ref=packed.at[near_index(i)],
            dst_ref=received.at[me_near],
            send_sem=data_send,
            recv_sem=data_recv,
            device_id={"brick": near_peer(i)},
            device_id_type=MESH,
        ).start()
    received[me_near] = packed[me_near]
    others_of(received, near, data_recv).wait()

    rows_of = jnp.dot(
        pick, received[...].reshape(near * 2 * held, PIX), preferred_element_type=jnp.float32
    )
    slot = iota((2 * SLOTS, PIX), 0) & (SLOTS - 1)
    for s in range(SLOTS):
        lhs[:, s * PIX : (s + 1) * PIX] = jnp.where(slot == s, rows_of, 0.0).astype(jnp.bfloat16)
    for copy in splits:
        copy.wait()

    def over_copy(side, half, step, owner):
        return pltpu.make_async_remote_copy(
            src_ref=over_send.at[side, half],
            dst_ref=over_recv.at[half, me_f],
            send_sem=over_send_sem.at[side],
            recv_sem=over_sem,
            device_id={"frame": owner, "brick": brick_peer(step)},
            device_id_type=MESH,
        )

    parts = WIDTH // PIX
    for half in range(HALVES):
        columns = pl.ds(half * WIDTH, WIDTH)
        contrib = jnp.dot(lhs[...], split[:, columns], preferred_element_type=jnp.float32)
        first = contrib.astype(jnp.bfloat16)
        left = contrib - first.astype(jnp.float32)
        second = left.astype(jnp.bfloat16)
        third = (left - second.astype(jnp.float32)).astype(jnp.bfloat16)
        acc[half] = jnp.dot(
            placer[...],
            jnp.concatenate([first, second, third], axis=0),
            preferred_element_type=jnp.float32,
        )

        for side in range(2):
            for c in range(2):
                for n in range(parts):
                    over_send[side, half, pl.ds(c * parts + n, 1), :] = acc[
                        half, pl.ds(2 * inner + c * 8 + side, 1), pl.ds(n * PIX, PIX)
                    ]

        @pl.when(me_b > 0)
        def _():
            over_copy(0, half, bricks - 1, groups - 1).start()

        @pl.when(me_b < bricks - 1)
        def _():
            over_copy(1, half, 1, 0).start()

        sums = acc[half, pl.ds(0, 2 * inner), :].reshape(2 * groups, ROWS_DEV, WIDTH)
        top = jnp.max(jnp.abs(sums), axis=1, keepdims=True)
        unit = jnp.where(top > 0.0, LEVELS / jnp.maximum(top, 1e-33), 0.0)
        code = jnp.round(sums * unit).astype(jnp.int32).astype(jnp.int16)
        coded[half] = code.reshape(2 * inner, WIDTH)
        top = top * (1.0 / LEVELS)
        for g in range(groups):
            for c in range(2):
                for n in range(parts):
                    scale[half, g, pl.ds(c * parts + n, 1), :] = top[
                        2 * g + c, :, n * PIX : (n + 1) * PIX
                    ]

        for i in range(1, groups):
            peer = frame_peer(i)
            pltpu.make_async_remote_copy(
                src_ref=scale.at[half, peer],
                dst_ref=scales.at[half, me_f],
                send_sem=scale_send.at[half],
                recv_sem=scale_recv.at[half],
                device_id={"frame": peer},
                device_id_type=MESH,
            ).start()
            pltpu.make_async_remote_copy(
                src_ref=coded.at[half, pl.ds(peer * 2 * ROWS_DEV, 2 * ROWS_DEV)],
                dst_ref=partial.at[half, me_f],
                send_sem=sum_send.at[half],
                recv_sem=sum_recv.at[half],
                device_id={"frame": peer},
                device_id_type=MESH,
            ).start()
        partial[half, me_f] = jnp.zeros((2 * ROWS_DEV, WIDTH), jnp.int16)
        scales[half, me_f] = jnp.zeros((2 * parts, PIX), jnp.float32)
        total[:, columns] = acc[
            half, pl.ds(pl.multiple_of(me_f * 2 * ROWS_DEV, 2 * ROWS_DEV), 2 * ROWS_DEV), :
        ]

    for half in range(HALVES):
        others = partial.at[half, pl.ds(0, groups - 1)]
        pltpu.make_async_copy(others, others, sum_recv.at[half]).wait()
        others = scales.at[half, pl.ds(0, groups - 1)]
        pltpu.make_async_copy(others, others, scale_recv.at[half]).wait()
        for c in range(2):
            for n in range(parts):
                where = (pl.ds(c * ROWS_DEV, ROWS_DEV), pl.ds(half * WIDTH + n * PIX, PIX))
                value = total[where]
                for g in range(groups):
                    term = partial[
                        half, g, pl.ds(c * ROWS_DEV, ROWS_DEV), pl.ds(n * PIX, PIX)
                    ]
                    value = value + term.astype(jnp.float32) * scales[half, g, pl.ds(c * parts + n, 1), :]
                total[where] = value

    def take_overhang(at):
        pltpu.make_async_copy(over_recv, over_recv, over_sem).wait()
        for half in range(HALVES):
            value = over_recv[half, 0]
            for g in range(1, groups):
                value = value + over_recv[half, g]
            for c in range(2):
                for n in range(parts):
                    where = (pl.ds(c * ROWS_DEV + at, 1), pl.ds(half * WIDTH + n * PIX, PIX))
                    total[where] = total[where] + value[c * parts + n : c * parts + n + 1]

    @pl.when((me_f == groups - 1) & (me_b < bricks - 1))
    def _():
        take_overhang(ROWS_DEV - 1)

    @pl.when((me_f == 0) & (me_b > 0))
    def _():
        take_overhang(0)

    others_of(pixels, FAR, pix_send).wait()
    others_of(request, near, req_send).wait()
    others_of(packed, near, data_send).wait()
    for half in range(HALVES):
        others = partial.at[half, pl.ds(0, groups - 1)]
        pltpu.make_async_copy(others, others, sum_send.at[half]).wait()
        others = scales.at[half, pl.ds(0, groups - 1)]
        pltpu.make_async_copy(others, others, scale_send.at[half]).wait()

    def sent_over(side):
        pltpu.make_async_copy(over_send.at[side], over_send.at[side], over_send_sem.at[side]).wait()

    @pl.when(me_b > 0)
    def _():
        sent_over(0)

    @pl.when(me_b < bricks - 1)
    def _():
        sent_over(1)


def on_device(intensity, correction, splitting, block_count, pix_index, vox_offset):
    bricks = lax.axis_size("brick")
    groups = lax.axis_size("frame")
    near = bricks // FAR
    message = 2 * CAP * FAR
    rows = 2 * groups * ROWS_DEV + 16
    hbm = pl.BlockSpec(memory_space=pltpu.HBM)
    dma = pltpu.SemaphoreType.DMA
    total = pl.pallas_call(
        functools.partial(kernel, bricks, groups),
        out_shape=jax.ShapeDtypeStruct((2 * ROWS_DEV, VOX), jnp.float32),
        in_specs=[hbm] * 6,
        out_specs=pl.BlockSpec(memory_space=pltpu.VMEM),
        scratch_shapes=[
            pltpu.SMEM((FR_DEV, 1, MAXB), jnp.int32),
            pltpu.SMEM((FR_DEV, 1, MAXB), jnp.int32),
            pltpu.SMEM((FR_DEV,), jnp.int32),
            pltpu.VMEM((FR_DEV, PB_DEV, PIX), jnp.float32),
            pltpu.VMEM((FR_DEV, PB_DEV, PIX), jnp.float32),
            pltpu.VMEM((SLOTS * PIX, VOX), jnp.bfloat16),
            pltpu.VMEM((FAR, 2 * FR_DEV * PB_DEV, PIX), jnp.bfloat16),
            pltpu.VMEM((near, 1, PIX), jnp.int32),
            pltpu.VMEM((near, message, PIX), jnp.bfloat16),
            pltpu.VMEM((near, message, PIX), jnp.bfloat16),
            pltpu.VMEM((2 * SLOTS, SLOTS * PIX), jnp.bfloat16),
            pltpu.VMEM((rows, 6 * SLOTS), jnp.bfloat16),
            pltpu.VMEM((HALVES, rows, WIDTH), jnp.float32),
            pltpu.VMEM((HALVES, 2 * groups * ROWS_DEV, WIDTH), jnp.int16),
            pltpu.VMEM((HALVES, groups, 2 * ROWS_DEV, WIDTH), jnp.int16),
            pltpu.VMEM((HALVES, groups, 2 * WIDTH // PIX, PIX), jnp.float32),
            pltpu.VMEM((HALVES, groups, 2 * WIDTH // PIX, PIX), jnp.float32),
            pltpu.VMEM((2, HALVES, 2 * WIDTH // PIX, PIX), jnp.float32),
            pltpu.VMEM((HALVES, groups, 2 * WIDTH // PIX, PIX), jnp.float32),
            dma((5,)),
            dma((CHUNKS,)),
            dma,
            dma,
            dma,
            dma,
            dma,
            dma,
            dma((HALVES,)),
            dma((HALVES,)),
            dma((HALVES,)),
            dma((HALVES,)),
            dma((2,)),
            dma,
        ],
        compiler_params=pltpu.CompilerParams(
            collective_id=0, has_side_effects=True, vmem_limit_bytes=32 * 1024 * 1024
        ),
    )(
        *[
            pltpu.with_memory_space_constraint(x, pltpu.HBM)
            for x in (
                pix_index,
                vox_offset,
                block_count.reshape(FR_DEV),
                intensity,
                correction,
                splitting.reshape(SLOTS * PIX, VOX),
            )
        ]
    )
    weight = total[ROWS_DEV:]
    merged = total[:ROWS_DEV] / jnp.maximum(weight, 1.0)
    return (merged[None], weight[None])


def solution(mesh):
    placed = (
        P("frame", "brick", None),
        P("frame", "brick", None),
        P("frame", "brick", None, None, None),
        P("frame", "brick"),
        P("frame", "brick", None),
        P("frame", "brick", None),
    )
    return jax.shard_map(
        on_device,
        mesh=mesh,
        in_specs=placed,
        out_specs=(P("brick", "frame", None), P("brick", "frame", None)),
        check_vma=False,
    )
```

```python
import functools

import jax
import jax.numpy as jnp
from jax import lax
from jax.experimental import pallas as pl
from jax.experimental.pallas import tpu as pltpu
from jax.sharding import PartitionSpec as P

MESH = pl.DeviceIdType.MESH
CAP = 4
FR_DEV = 4
MAXB = 8
PB_DEV = 16
ROWS_DEV = 16
SLOTS = FR_DEV * MAXB
PIX = 128
VOX = 512
HALVES = 1
WIDTH = VOX // HALVES
CHUNKS = 4
LEVELS = 32767.0
FAR = 4


def iota(shape, dim):
    return lax.broadcasted_iota(jnp.int32, shape, dim)


def kernel(
    bricks,
    groups,
    pix_hbm,
    vox_hbm,
    count_hbm,
    intensity_hbm,
    correction_hbm,
    split_hbm,
    total,
    pix_ref,
    vox_ref,
    count_ref,
    inten,
    corr,
    split,
    pixels,
    request,
    packed,
    received,
    lhs,
    placer,
    acc,
    coded,
    partial,
    scale,
    scales,
    over_send,
    over_recv,
    load_sem,
    split_sem,
    pix_send,
    pix_recv,
    met,
    req_send,
    req_recv,
    data_send,
    data_recv,
    sum_send,
    sum_recv,
    scale_send,
    scale_recv,
    over_send_sem,
    over_sem,
):
    me_f = lax.axis_index("frame")
    me_b = lax.axis_index("brick")
    near = bricks // FAR
    me_y = me_b // (2 * FAR)
    me_c = lax.rem(me_b, 2)
    me_far = lax.rem(me_b // 2, FAR)
    me_near = me_y * 2 + me_c
    held = CAP * FAR
    barrier = pltpu.get_barrier_semaphore()

    def brick_peer(i):
        return lax.rem(me_b + i, bricks)

    def brick_of(at_near, at_far):
        return (at_near // 2 * FAR + at_far) * 2 + lax.rem(at_near, 2)

    order = sorted(range(1, near), key=lambda i: (-min(i, near - i), i))

    def near_index(i):
        return lax.rem(me_near + i, near)

    def near_peer(i):
        return brick_of(near_index(i), me_far)

    def far_peer(i):
        return brick_of(me_near, lax.rem(me_far + i, FAR))

    line = groups // 2
    me_line = me_f // line
    other_core = me_b + 1 - 2 * lax.rem(me_b, 2)

    def line_peer(i):
        return me_line * line + lax.rem(me_f + i, line)

    def frame_peer(i):
        return lax.rem(me_f + i, groups)

    for i in range(1, FAR):
        pl.semaphore_signal(
            barrier, inc=1, device_id={"brick": far_peer(i)}, device_id_type=MESH
        )
    for i in range(2, near, 2):
        pl.semaphore_signal(
            barrier, inc=1, device_id={"brick": near_peer(i)}, device_id_type=MESH
        )
    pl.semaphore_signal(barrier, inc=1, device_id={"brick": other_core}, device_id_type=MESH)
    for i in range(1, line):
        pl.semaphore_signal(
            barrier, inc=1, device_id={"frame": line_peer(i)}, device_id_type=MESH
        )
    pl.semaphore_signal(
        barrier, inc=1, device_id={"frame": frame_peer(line)}, device_id_type=MESH
    )

    @pl.when((me_f == 0) | (me_f == groups - 1))
    def _():
        for i in range(1, line):
            pl.semaphore_signal(
                barrier,
                inc=1,
                device_id={"frame": (1 - me_line) * line + lax.rem(me_f + i, line)},
                device_id_type=MESH,
            )

    tables = [
        pltpu.make_async_copy(pix_hbm, pix_ref, load_sem.at[0]),
        pltpu.make_async_copy(vox_hbm, vox_ref, load_sem.at[1]),
        pltpu.make_async_copy(count_hbm, count_ref, load_sem.at[2]),
    ]
    loads = [
        pltpu.make_async_copy(intensity_hbm, inten, load_sem.at[3]),
        pltpu.make_async_copy(correction_hbm, corr, load_sem.at[4]),
    ]
    depth = SLOTS * PIX // CHUNKS
    splits = [
        pltpu.make_async_copy(
            split_hbm.at[pl.ds(k * depth, depth)],
            split.at[pl.ds(k * depth, depth)],
            split_sem.at[k],
        )
        for k in range(CHUNKS)
    ]
    for copy in tables + loads + splits:
        copy.start()
    for copy in tables:
        copy.wait()

    lane = iota((1, PIX), 1)
    row = jnp.full((1, PIX), -1, jnp.int32)
    for s in range(SLOTS):
        row = jnp.where(lane == s, pix_ref[s // MAXB, 0, s % MAXB], row)
    sub2, lane2 = iota((SLOTS, PIX), 0), iota((SLOTS, PIX), 1)
    column = jnp.sum(
        jnp.where(sub2 == lane2, jnp.broadcast_to(row, (SLOTS, PIX)), 0), axis=1, keepdims=True
    )
    near_row = (row // (2 * FAR * PB_DEV)) * 2 + ((row >> 4) & 1)
    near_col = (column // (2 * FAR * PB_DEV)) * 2 + ((column >> 4) & 1)
    same = (jnp.broadcast_to(near_row, (SLOTS, PIX)) == near_col).astype(jnp.int32)
    rank_row = jnp.sum(jnp.where(sub2 < lane2, same, 0), axis=0, keepdims=True)
    rank_col = jnp.sum(jnp.where(lane2 < sub2, same, 0), axis=1, keepdims=True)
    where_row = ((row >> 5) & (FAR - 1)) * 128 + (lane >> 3) * PB_DEV + (row & 15)
    code = (near_row * held + rank_row) * 1024 + where_row
    request[me_near] = jnp.where(lane < SLOTS, code, -1)
    key = near_col * held + rank_col
    wide = iota((SLOTS, near * 2 * held), 1)
    pick = jnp.concatenate(
        [jnp.where(wide == key * 2 + c, 1.0, 0.0).astype(jnp.float32) for c in range(2)],
        axis=0,
    ).astype(jnp.bfloat16)

    inner = groups * ROWS_DEV
    rows = 2 * inner + 16
    pieces = 3
    wide_lane = iota((1, pieces * 2 * SLOTS), 1)
    voxel = jnp.full((1, pieces * 2 * SLOTS), -1, jnp.int32)
    for s in range(SLOTS):
        f, m = s // MAXB, s % MAXB
        offset = vox_ref[f, 0, m]
        target = jnp.where(offset == 0, inner, jnp.where(offset == inner + 1, inner + 1, offset - 1))
        target = jnp.where(m < count_ref[f], target, -1)
        voxel = jnp.where((wide_lane & (SLOTS - 1)) == s, target, voxel)
    down = iota((rows, pieces * 2 * SLOTS), 0)
    tail = down >= 2 * inner
    own_voxel = jnp.where(tail, inner + (down & 7), (down >> 5) * ROWS_DEV + (down & 15))
    own_channel = jnp.where(tail, (down >> 3) & 1, (down >> 4) & 1)
    channel = (iota((rows, pieces * 2 * SLOTS), 1) // SLOTS) & 1
    hit = (own_voxel == voxel) & (own_channel == channel)
    placer[...] = jnp.where(hit, 1.0, 0.0).astype(jnp.float32).astype(jnp.bfloat16)

    for copy in loads:
        copy.wait()
    pixels[me_far] = jnp.concatenate(
        [inten[...].reshape(FR_DEV * PB_DEV, PIX), corr[...].reshape(FR_DEV * PB_DEV, PIX)],
        axis=0,
    ).astype(jnp.bfloat16)

    ends = jnp.where((me_f == line - 1) | (me_f == line), 0, 1)
    pl.semaphore_wait(barrier, FAR - 1 + near // 2 - 1 + 1 + line - 1 + 1 + ends)
    pl.semaphore_signal(met.at[0], inc=1, device_id={"brick": other_core}, device_id_type=MESH)
    pl.semaphore_signal(
        met.at[1], inc=1, device_id={"frame": frame_peer(line)}, device_id_type=MESH
    )

    def push(i):
        pltpu.make_async_remote_copy(
            src_ref=pixels.at[me_far],
            dst_ref=pixels.at[me_far],
            send_sem=pix_send,
            recv_sem=pix_recv,
            device_id={"brick": far_peer(i)},
            device_id_type=MESH,
        ).start()

    for i in range(FAR - 1, 0, -1):

        @pl.when(me_far >= i)
        def _():
            push(FAR - i)

    for i in range(FAR - 1, 0, -1):

        @pl.when(me_far + i < FAR)
        def _():
            push(i)

    pl.semaphore_wait(met.at[0], 1)
    pl.semaphore_wait(met.at[1], 1)
    for i in order:
        pltpu.make_async_remote_copy(
            src_ref=request.at[me_near],
            dst_ref=request.at[me_near],
            send_sem=req_send,
            recv_sem=req_recv,
            device_id={"brick": near_peer(i)},
            device_id_type=MESH,
        ).start()

    def others_of(buffer, count, sem):
        others = buffer.at[pl.ds(0, count - 1)]
        return pltpu.make_async_copy(others, others, sem)

    others_of(request, near, req_recv).wait()

    asked = jnp.concatenate(
        [jnp.broadcast_to(request[d], (2 * held, PIX)) for d in range(near)], axis=0
    )
    place = lax.rem(iota((near * 2 * held, PIX), 0), 2 * held)
    wanted = (asked >> 10) == me_near * held + (place >> 1)
    found = jnp.sum(jnp.where(wanted, (asked & 1023) + 1, 0), axis=1, keepdims=True)
    spot = jnp.where(found > 0, found - 1 + (place[:, 0:1] & 1) * 64, -1)
    select = jnp.where(iota((near * 2 * held, FAR * PIX), 1) == spot, 1.0, 0.0)
    select = select.astype(jnp.float32).astype(jnp.bfloat16)

    others_of(pixels, FAR, pix_recv).wait()
    blocks = jnp.dot(
        select, pixels[...].reshape(FAR * PIX, PIX), preferred_element_type=jnp.float32
    ).astype(jnp.bfloat16)
    packed[...] = blocks.reshape(near, 2 * held, PIX)

    for i in order:
        pltpu.make_async_remote_copy(
            src_ref=packed.at[near_index(i)],
            dst_ref=received.at[me_near],
            send_sem=data_send,
            recv_sem=data_recv,
            device_id={"brick": near_peer(i)},
            device_id_type=MESH,
        ).start()
    received[me_near] = packed[me_near]
    others_of(received, near, data_recv).wait()

    rows_of = jnp.dot(
        pick, received[...].reshape(near * 2 * held, PIX), preferred_element_type=jnp.float32
    )
    slot = iota((2 * SLOTS, PIX), 0) & (SLOTS - 1)
    for s in range(SLOTS):
        lhs[:, s * PIX : (s + 1) * PIX] = jnp.where(slot == s, rows_of, 0.0).astype(jnp.bfloat16)
    for copy in splits:
        copy.wait()

    def over_copy(side, half, step, owner):
        return pltpu.make_async_remote_copy(
            src_ref=over_send.at[side, half],
            dst_ref=over_recv.at[half, me_f],
            send_sem=over_send_sem.at[side],
            recv_sem=over_sem,
            device_id={"frame": owner, "brick": brick_peer(step)},
            device_id_type=MESH,
        )

    parts = WIDTH // PIX
    for half in range(HALVES):
        columns = pl.ds(half * WIDTH, WIDTH)
        contrib = jnp.dot(lhs[...], split[:, columns], preferred_element_type=jnp.float32)
        first = contrib.astype(jnp.bfloat16)
        left = contrib - first.astype(jnp.float32)
        second = left.astype(jnp.bfloat16)
        third = (left - second.astype(jnp.float32)).astype(jnp.bfloat16)
        acc[half] = jnp.dot(
            placer[...],
            jnp.concatenate([first, second, third], axis=0),
            preferred_element_type=jnp.float32,
        )

        for side in range(2):
            for c in range(2):
                for n in range(parts):
                    over_send[side, half, pl.ds(c * parts + n, 1), :] = acc[
                        half, pl.ds(2 * inner + c * 8 + side, 1), pl.ds(n * PIX, PIX)
                    ]

        @pl.when(me_b > 0)
        def _():
            over_copy(0, half, bricks - 1, groups - 1).start()

        @pl.when(me_b < bricks - 1)
        def _():
            over_copy(1, half, 1, 0).start()

        sums = acc[half, pl.ds(0, 2 * inner), :].reshape(2 * groups, ROWS_DEV, WIDTH)
        top = jnp.max(jnp.abs(sums), axis=1, keepdims=True)
        unit = jnp.where(top > 0.0, LEVELS / jnp.maximum(top, 1e-33), 0.0)
        code = jnp.round(sums * unit).astype(jnp.int32).astype(jnp.int16)
        coded[half] = code.reshape(2 * inner, WIDTH)
        top = top * (1.0 / LEVELS)
        for g in range(groups):
            for c in range(2):
                for n in range(parts):
                    scale[half, g, pl.ds(c * parts + n, 1), :] = top[
                        2 * g + c, :, n * PIX : (n + 1) * PIX
                    ]

        for i in range(1, groups):
            peer = frame_peer(i)
            pltpu.make_async_remote_copy(
                src_ref=scale.at[half, peer],
                dst_ref=scales.at[half, me_f],
                send_sem=scale_send.at[half],
                recv_sem=scale_recv.at[half],
                device_id={"frame": peer},
                device_id_type=MESH,
            ).start()
            pltpu.make_async_remote_copy(
                src_ref=coded.at[half, pl.ds(peer * 2 * ROWS_DEV, 2 * ROWS_DEV)],
                dst_ref=partial.at[half, me_f],
                send_sem=sum_send.at[half],
                recv_sem=sum_recv.at[half],
                device_id={"frame": peer},
                device_id_type=MESH,
            ).start()
        partial[half, me_f] = jnp.zeros((2 * ROWS_DEV, WIDTH), jnp.int16)
        scales[half, me_f] = jnp.zeros((2 * parts, PIX), jnp.float32)
        total[:, columns] = acc[
            half, pl.ds(pl.multiple_of(me_f * 2 * ROWS_DEV, 2 * ROWS_DEV), 2 * ROWS_DEV), :
        ]

    for half in range(HALVES):
        others = partial.at[half, pl.ds(0, groups - 1)]
        pltpu.make_async_copy(others, others, sum_recv.at[half]).wait()
        others = scales.at[half, pl.ds(0, groups - 1)]
        pltpu.make_async_copy(others, others, scale_recv.at[half]).wait()
        for c in range(2):
            for n in range(parts):
                where = (pl.ds(c * ROWS_DEV, ROWS_DEV), pl.ds(half * WIDTH + n * PIX, PIX))
                value = total[where]
                for g in range(groups):
                    term = partial[
                        half, g, pl.ds(c * ROWS_DEV, ROWS_DEV), pl.ds(n * PIX, PIX)
                    ]
                    value = value + term.astype(jnp.float32) * scales[half, g, pl.ds(c * parts + n, 1), :]
                total[where] = value

    def take_overhang(at):
        pltpu.make_async_copy(over_recv, over_recv, over_sem).wait()
        for half in range(HALVES):
            value = over_recv[half, 0]
            for g in range(1, groups):
                value = value + over_recv[half, g]
            for c in range(2):
                for n in range(parts):
                    where = (pl.ds(c * ROWS_DEV + at, 1), pl.ds(half * WIDTH + n * PIX, PIX))
                    total[where] = total[where] + value[c * parts + n : c * parts + n + 1]

    @pl.when((me_f == groups - 1) & (me_b < bricks - 1))
    def _():
        take_overhang(ROWS_DEV - 1)

    @pl.when((me_f == 0) & (me_b > 0))
    def _():
        take_overhang(0)

    others_of(pixels, FAR, pix_send).wait()
    others_of(request, near, req_send).wait()
    others_of(packed, near, data_send).wait()
    for half in range(HALVES):
        others = partial.at[half, pl.ds(0, groups - 1)]
        pltpu.make_async_copy(others, others, sum_send.at[half]).wait()
        others = scales.at[half, pl.ds(0, groups - 1)]
        pltpu.make_async_copy(others, others, scale_send.at[half]).wait()

    def sent_over(side):
        pltpu.make_async_copy(over_send.at[side], over_send.at[side], over_send_sem.at[side]).wait()

    @pl.when(me_b > 0)
    def _():
        sent_over(0)

    @pl.when(me_b < bricks - 1)
    def _():
        sent_over(1)


def on_device(intensity, correction, splitting, block_count, pix_index, vox_offset):
    bricks = lax.axis_size("brick")
    groups = lax.axis_size("frame")
    near = bricks // FAR
    message = 2 * CAP * FAR
    rows = 2 * groups * ROWS_DEV + 16
    hbm = pl.BlockSpec(memory_space=pltpu.HBM)
    dma = pltpu.SemaphoreType.DMA
    total = pl.pallas_call(
        functools.partial(kernel, bricks, groups),
        out_shape=jax.ShapeDtypeStruct((2 * ROWS_DEV, VOX), jnp.float32),
        in_specs=[hbm] * 6,
        out_specs=pl.BlockSpec(memory_space=pltpu.VMEM),
        scratch_shapes=[
            pltpu.SMEM((FR_DEV, 1, MAXB), jnp.int32),
            pltpu.SMEM((FR_DEV, 1, MAXB), jnp.int32),
            pltpu.SMEM((FR_DEV,), jnp.int32),
            pltpu.VMEM((FR_DEV, PB_DEV, PIX), jnp.float32),
            pltpu.VMEM((FR_DEV, PB_DEV, PIX), jnp.float32),
            pltpu.VMEM((SLOTS * PIX, VOX), jnp.bfloat16),
            pltpu.VMEM((FAR, 2 * FR_DEV * PB_DEV, PIX), jnp.bfloat16),
            pltpu.VMEM((near, 1, PIX), jnp.int32),
            pltpu.VMEM((near, message, PIX), jnp.bfloat16),
            pltpu.VMEM((near, message, PIX), jnp.bfloat16),
            pltpu.VMEM((2 * SLOTS, SLOTS * PIX), jnp.bfloat16),
            pltpu.VMEM((rows, 6 * SLOTS), jnp.bfloat16),
            pltpu.VMEM((HALVES, rows, WIDTH), jnp.float32),
            pltpu.VMEM((HALVES, 2 * groups * ROWS_DEV, WIDTH), jnp.int16),
            pltpu.VMEM((HALVES, groups, 2 * ROWS_DEV, WIDTH), jnp.int16),
            pltpu.VMEM((HALVES, groups, 2 * WIDTH // PIX, PIX), jnp.float32),
            pltpu.VMEM((HALVES, groups, 2 * WIDTH // PIX, PIX), jnp.float32),
            pltpu.VMEM((2, HALVES, 2 * WIDTH // PIX, PIX), jnp.float32),
            pltpu.VMEM((HALVES, groups, 2 * WIDTH // PIX, PIX), jnp.float32),
            dma((5,)),
            dma((CHUNKS,)),
            dma,
            dma,
            pltpu.SemaphoreType.REGULAR((2,)),
            dma,
            dma,
            dma,
            dma,
            dma((HALVES,)),
            dma((HALVES,)),
            dma((HALVES,)),
            dma((HALVES,)),
            dma((2,)),
            dma,
        ],
        compiler_params=pltpu.CompilerParams(
            collective_id=0, has_side_effects=True, vmem_limit_bytes=32 * 1024 * 1024
        ),
    )(
        *[
            pltpu.with_memory_space_constraint(x, pltpu.HBM)
            for x in (
                pix_index,
                vox_offset,
                block_count.reshape(FR_DEV),
                intensity,
                correction,
                splitting.reshape(SLOTS * PIX, VOX),
            )
        ]
    )
    weight = total[ROWS_DEV:]
    merged = total[:ROWS_DEV] / jnp.maximum(weight, 1.0)
    return (merged[None], weight[None])


def solution(mesh):
    placed = (
        P("frame", "brick", None),
        P("frame", "brick", None),
        P("frame", "brick", None, None, None),
        P("frame", "brick"),
        P("frame", "brick", None),
        P("frame", "brick", None),
    )
    return jax.shard_map(
        on_device,
        mesh=mesh,
        in_specs=placed,
        out_specs=(P("brick", "frame", None), P("brick", "frame", None)),
        check_vma=False,
    )
```

```python
import functools

import jax
import jax.numpy as jnp
from jax import lax
from jax.experimental import pallas as pl
from jax.experimental.pallas import tpu as pltpu
from jax.sharding import PartitionSpec as P

MESH = pl.DeviceIdType.MESH
CAP = 4
FR_DEV = 4
MAXB = 8
PB_DEV = 16
ROWS_DEV = 16
SLOTS = FR_DEV * MAXB
PIX = 128
VOX = 512
HALVES = 1
WIDTH = VOX // HALVES
CHUNKS = 4
LEVELS = 32767.0
FAR = 4


def iota(shape, dim):
    return lax.broadcasted_iota(jnp.int32, shape, dim)


def kernel(
    bricks,
    groups,
    pix_hbm,
    vox_hbm,
    count_hbm,
    intensity_hbm,
    correction_hbm,
    split_hbm,
    total,
    pix_ref,
    vox_ref,
    count_ref,
    inten,
    corr,
    split,
    pixels,
    request,
    packed,
    received,
    lhs,
    placer,
    acc,
    coded,
    partial,
    scale,
    scales,
    over_send,
    over_recv,
    load_sem,
    split_sem,
    pix_send,
    pix_recv,
    met,
    req_send,
    req_recv,
    data_send,
    data_recv,
    sum_send,
    sum_recv,
    scale_send,
    scale_recv,
    over_send_sem,
    over_sem,
):
    me_f = lax.axis_index("frame")
    me_b = lax.axis_index("brick")
    near = bricks // FAR
    me_y = me_b // (2 * FAR)
    me_c = lax.rem(me_b, 2)
    me_far = lax.rem(me_b // 2, FAR)
    me_near = me_y * 2 + me_c
    held = CAP * FAR
    barrier = pltpu.get_barrier_semaphore()

    def brick_peer(i):
        return lax.rem(me_b + i, bricks)

    def brick_of(at_near, at_far):
        return (at_near // 2 * FAR + at_far) * 2 + lax.rem(at_near, 2)

    order = sorted(range(1, near), key=lambda i: (-min(i, near - i), i))

    def near_index(i):
        return lax.rem(me_near + i, near)

    def near_peer(i):
        return brick_of(near_index(i), me_far)

    def far_peer(i):
        return brick_of(me_near, lax.rem(me_far + i, FAR))

    line = groups // 2
    me_line = me_f // line
    other_core = me_b + 1 - 2 * lax.rem(me_b, 2)

    def line_peer(i):
        return me_line * line + lax.rem(me_f + i, line)

    def frame_peer(i):
        return lax.rem(me_f + i, groups)

    for i in range(1, FAR):
        pl.semaphore_signal(
            barrier, inc=1, device_id={"brick": far_peer(i)}, device_id_type=MESH
        )
    for i in range(2, near, 2):
        pl.semaphore_signal(
            barrier, inc=1, device_id={"brick": near_peer(i)}, device_id_type=MESH
        )
    pl.semaphore_signal(barrier, inc=1, device_id={"brick": other_core}, device_id_type=MESH)
    for i in range(1, line):
        pl.semaphore_signal(
            barrier, inc=1, device_id={"frame": line_peer(i)}, device_id_type=MESH
        )
    pl.semaphore_signal(
        barrier, inc=1, device_id={"frame": frame_peer(line)}, device_id_type=MESH
    )

    @pl.when((me_f == 0) | (me_f == groups - 1))
    def _():
        for i in range(1, line):
            pl.semaphore_signal(
                barrier,
                inc=1,
                device_id={"frame": (1 - me_line) * line + lax.rem(me_f + i, line)},
                device_id_type=MESH,
            )

    tables = [
        pltpu.make_async_copy(pix_hbm, pix_ref, load_sem.at[0]),
        pltpu.make_async_copy(vox_hbm, vox_ref, load_sem.at[1]),
        pltpu.make_async_copy(count_hbm, count_ref, load_sem.at[2]),
    ]
    loads = [
        pltpu.make_async_copy(intensity_hbm, inten, load_sem.at[3]),
        pltpu.make_async_copy(correction_hbm, corr, load_sem.at[4]),
    ]
    depth = SLOTS * PIX // CHUNKS
    splits = [
        pltpu.make_async_copy(
            split_hbm.at[pl.ds(k * depth, depth)],
            split.at[pl.ds(k * depth, depth)],
            split_sem.at[k],
        )
        for k in range(CHUNKS)
    ]
    for copy in tables + loads + splits:
        copy.start()
    for copy in tables:
        copy.wait()

    lane = iota((1, PIX), 1)
    row = jnp.full((1, PIX), -1, jnp.int32)
    for s in range(SLOTS):
        row = jnp.where(lane == s, pix_ref[s // MAXB, 0, s % MAXB], row)
    sub2, lane2 = iota((SLOTS, PIX), 0), iota((SLOTS, PIX), 1)
    column = jnp.sum(
        jnp.where(sub2 == lane2, jnp.broadcast_to(row, (SLOTS, PIX)), 0), axis=1, keepdims=True
    )
    near_row = (row // (2 * FAR * PB_DEV)) * 2 + ((row >> 4) & 1)
    near_col = (column // (2 * FAR * PB_DEV)) * 2 + ((column >> 4) & 1)
    same = (jnp.broadcast_to(near_row, (SLOTS, PIX)) == near_col).astype(jnp.int32)
    rank_row = jnp.sum(jnp.where(sub2 < lane2, same, 0), axis=0, keepdims=True)
    rank_col = jnp.sum(jnp.where(lane2 < sub2, same, 0), axis=1, keepdims=True)
    where_row = ((row >> 5) & (FAR - 1)) * 128 + (lane >> 3) * PB_DEV + (row & 15)
    code = (near_row * held + rank_row) * 1024 + where_row
    request[me_near] = jnp.where(lane < SLOTS, code, -1)
    key = near_col * held + rank_col
    wide = iota((SLOTS, near * 2 * held), 1)
    pick = jnp.concatenate(
        [jnp.where(wide == key * 2 + c, 1.0, 0.0).astype(jnp.float32) for c in range(2)],
        axis=0,
    ).astype(jnp.bfloat16)

    inner = groups * ROWS_DEV
    rows = 2 * inner + 16
    pieces = 3
    wide_lane = iota((1, pieces * 2 * SLOTS), 1)
    voxel = jnp.full((1, pieces * 2 * SLOTS), -1, jnp.int32)
    for s in range(SLOTS):
        f, m = s // MAXB, s % MAXB
        offset = vox_ref[f, 0, m]
        target = jnp.where(offset == 0, inner, jnp.where(offset == inner + 1, inner + 1, offset - 1))
        target = jnp.where(m < count_ref[f], target, -1)
        voxel = jnp.where((wide_lane & (SLOTS - 1)) == s, target, voxel)
    down = iota((rows, pieces * 2 * SLOTS), 0)
    tail = down >= 2 * inner
    own_voxel = jnp.where(tail, inner + (down & 7), (down >> 5) * ROWS_DEV + (down & 15))
    own_channel = jnp.where(tail, (down >> 3) & 1, (down >> 4) & 1)
    channel = (iota((rows, pieces * 2 * SLOTS), 1) // SLOTS) & 1
    hit = (own_voxel == voxel) & (own_channel == channel)
    placer[...] = jnp.where(hit, 1.0, 0.0).astype(jnp.float32).astype(jnp.bfloat16)

    for copy in loads:
        copy.wait()
    pixels[me_far] = jnp.concatenate(
        [inten[...].reshape(FR_DEV * PB_DEV, PIX), corr[...].reshape(FR_DEV * PB_DEV, PIX)],
        axis=0,
    ).astype(jnp.bfloat16)

    ends = jnp.where((me_f == line - 1) | (me_f == line), 0, 1)
    pl.semaphore_wait(barrier, FAR - 1 + near // 2 - 1 + 1 + line - 1 + 1 + ends)
    pl.semaphore_signal(met.at[0], inc=1, device_id={"brick": other_core}, device_id_type=MESH)
    pl.semaphore_signal(
        met.at[1], inc=1, device_id={"frame": frame_peer(line)}, device_id_type=MESH
    )

    def push(i):
        pltpu.make_async_remote_copy(
            src_ref=pixels.at[me_far],
            dst_ref=pixels.at[me_far],
            send_sem=pix_send,
            recv_sem=pix_recv,
            device_id={"brick": far_peer(i)},
            device_id_type=MESH,
        ).start()

    for i in range(FAR - 1, 0, -1):

        @pl.when(me_far >= i)
        def _():
            push(FAR - i)

    for i in range(FAR - 1, 0, -1):

        @pl.when(me_far + i < FAR)
        def _():
            push(i)

    pl.semaphore_wait(met.at[0], 1)
    pl.semaphore_wait(met.at[1], 1)
    for i in order:
        pltpu.make_async_remote_copy(
            src_ref=request.at[me_near],
            dst_ref=request.at[me_near],
            send_sem=req_send,
            recv_sem=req_recv,
            device_id={"brick": near_peer(i)},
            device_id_type=MESH,
        ).start()

    def others_of(buffer, count, sem):
        others = buffer.at[pl.ds(0, count - 1)]
        return pltpu.make_async_copy(others, others, sem)

    others_of(request, near, req_recv).wait()

    asked = jnp.concatenate(
        [jnp.broadcast_to(request[d], (2 * held, PIX)) for d in range(near)], axis=0
    )
    place = lax.rem(iota((near * 2 * held, PIX), 0), 2 * held)
    wanted = (asked >> 10) == me_near * held + (place >> 1)
    found = jnp.sum(jnp.where(wanted, (asked & 1023) + 1, 0), axis=1, keepdims=True)
    spot = jnp.where(found > 0, found - 1 + (place[:, 0:1] & 1) * 64, -1)
    select = jnp.where(iota((near * 2 * held, FAR * PIX), 1) == spot, 1.0, 0.0)
    select = select.astype(jnp.float32).astype(jnp.bfloat16)

    others_of(pixels, FAR, pix_recv).wait()
    blocks = jnp.dot(
        select, pixels[...].reshape(FAR * PIX, PIX), preferred_element_type=jnp.float32
    ).astype(jnp.bfloat16)
    packed[...] = blocks.reshape(near, 2 * held, PIX)

    for i in order:
        pltpu.make_async_remote_copy(
            src_ref=packed.at[near_index(i)],
            dst_ref=received.at[me_near],
            send_sem=data_send,
            recv_sem=data_recv,
            device_id={"brick": near_peer(i)},
            device_id_type=MESH,
        ).start()
    received[me_near] = packed[me_near]
    others_of(received, near, data_recv).wait()

    rows_of = jnp.dot(
        pick, received[...].reshape(near * 2 * held, PIX), preferred_element_type=jnp.float32
    )
    slot = iota((2 * SLOTS, PIX), 0) & (SLOTS - 1)
    for s in range(SLOTS):
        lhs[:, s * PIX : (s + 1) * PIX] = jnp.where(slot == s, rows_of, 0.0).astype(jnp.bfloat16)
    for copy in splits:
        copy.wait()

    def over_copy(side, half, step, owner):
        return pltpu.make_async_remote_copy(
            src_ref=over_send.at[side, half],
            dst_ref=over_recv.at[half, me_f],
            send_sem=over_send_sem.at[side],
            recv_sem=over_sem,
            device_id={"frame": owner, "brick": brick_peer(step)},
            device_id_type=MESH,
        )

    parts = WIDTH // PIX
    for half in range(HALVES):
        columns = pl.ds(half * WIDTH, WIDTH)
        contrib = jnp.dot(lhs[...], split[:, columns], preferred_element_type=jnp.float32)
        first = contrib.astype(jnp.bfloat16)
        left = contrib - first.astype(jnp.float32)
        second = left.astype(jnp.bfloat16)
        third = (left - second.astype(jnp.float32)).astype(jnp.bfloat16)
        acc[half] = jnp.dot(
            placer[...],
            jnp.concatenate([first, second, third], axis=0),
            preferred_element_type=jnp.float32,
        )

        for side in range(2):
            for c in range(2):
                for n in range(parts):
                    over_send[side, half, pl.ds(c * parts + n, 1), :] = acc[
                        half, pl.ds(2 * inner + c * 8 + side, 1), pl.ds(n * PIX, PIX)
                    ]

        @pl.when(me_b > 0)
        def _():
            over_copy(0, half, bricks - 1, groups - 1).start()

        @pl.when(me_b < bricks - 1)
        def _():
            over_copy(1, half, 1, 0).start()

        sums = acc[half, pl.ds(0, 2 * inner), :].reshape(2 * groups, ROWS_DEV, WIDTH)
        top = jnp.maximum(jnp.max(jnp.abs(sums), axis=1, keepdims=True), 1e-33)
        code = jnp.round(sums * (LEVELS / top)).astype(jnp.int32).astype(jnp.int16)
        coded[half] = code.reshape(2 * inner, WIDTH)
        top = top * (1.0 / LEVELS)
        for g in range(groups):
            for c in range(2):
                for n in range(parts):
                    scale[half, g, pl.ds(c * parts + n, 1), :] = top[
                        2 * g + c, :, n * PIX : (n + 1) * PIX
                    ]

        for i in range(1, groups):
            peer = frame_peer(i)
            pltpu.make_async_remote_copy(
                src_ref=scale.at[half, peer],
                dst_ref=scales.at[half, me_f],
                send_sem=scale_send.at[half],
                recv_sem=scale_recv.at[half],
                device_id={"frame": peer},
                device_id_type=MESH,
            ).start()
            pltpu.make_async_remote_copy(
                src_ref=coded.at[half, pl.ds(peer * 2 * ROWS_DEV, 2 * ROWS_DEV)],
                dst_ref=partial.at[half, me_f],
                send_sem=sum_send.at[half],
                recv_sem=sum_recv.at[half],
                device_id={"frame": peer},
                device_id_type=MESH,
            ).start()
        partial[half, me_f] = jnp.zeros((2 * ROWS_DEV, WIDTH), jnp.int16)
        scales[half, me_f] = jnp.zeros((2 * parts, PIX), jnp.float32)
        total[:, columns] = acc[
            half, pl.ds(pl.multiple_of(me_f * 2 * ROWS_DEV, 2 * ROWS_DEV), 2 * ROWS_DEV), :
        ]

    for half in range(HALVES):
        others = partial.at[half, pl.ds(0, groups - 1)]
        pltpu.make_async_copy(others, others, sum_recv.at[half]).wait()
        others = scales.at[half, pl.ds(0, groups - 1)]
        pltpu.make_async_copy(others, others, scale_recv.at[half]).wait()
        for c in range(2):
            for n in range(parts):
                where = (pl.ds(c * ROWS_DEV, ROWS_DEV), pl.ds(half * WIDTH + n * PIX, PIX))
                value = total[where]
                for g in range(groups):
                    term = partial[
                        half, g, pl.ds(c * ROWS_DEV, ROWS_DEV), pl.ds(n * PIX, PIX)
                    ]
                    value = value + term.astype(jnp.float32) * scales[half, g, pl.ds(c * parts + n, 1), :]
                total[where] = value

    def take_overhang(at):
        pltpu.make_async_copy(over_recv, over_recv, over_sem).wait()
        for half in range(HALVES):
            value = over_recv[half, 0]
            for g in range(1, groups):
                value = value + over_recv[half, g]
            for c in range(2):
                for n in range(parts):
                    where = (pl.ds(c * ROWS_DEV + at, 1), pl.ds(half * WIDTH + n * PIX, PIX))
                    total[where] = total[where] + value[c * parts + n : c * parts + n + 1]

    @pl.when((me_f == groups - 1) & (me_b < bricks - 1))
    def _():
        take_overhang(ROWS_DEV - 1)

    @pl.when((me_f == 0) & (me_b > 0))
    def _():
        take_overhang(0)

    others_of(pixels, FAR, pix_send).wait()
    others_of(request, near, req_send).wait()
    others_of(packed, near, data_send).wait()
    for half in range(HALVES):
        others = partial.at[half, pl.ds(0, groups - 1)]
        pltpu.make_async_copy(others, others, sum_send.at[half]).wait()
        others = scales.at[half, pl.ds(0, groups - 1)]
        pltpu.make_async_copy(others, others, scale_send.at[half]).wait()

    def sent_over(side):
        pltpu.make_async_copy(over_send.at[side], over_send.at[side], over_send_sem.at[side]).wait()

    @pl.when(me_b > 0)
    def _():
        sent_over(0)

    @pl.when(me_b < bricks - 1)
    def _():
        sent_over(1)


def on_device(intensity, correction, splitting, block_count, pix_index, vox_offset):
    bricks = lax.axis_size("brick")
    groups = lax.axis_size("frame")
    near = bricks // FAR
    message = 2 * CAP * FAR
    rows = 2 * groups * ROWS_DEV + 16
    hbm = pl.BlockSpec(memory_space=pltpu.HBM)
    dma = pltpu.SemaphoreType.DMA
    total = pl.pallas_call(
        functools.partial(kernel, bricks, groups),
        out_shape=jax.ShapeDtypeStruct((2 * ROWS_DEV, VOX), jnp.float32),
        in_specs=[hbm] * 6,
        out_specs=pl.BlockSpec(memory_space=pltpu.VMEM),
        scratch_shapes=[
            pltpu.SMEM((FR_DEV, 1, MAXB), jnp.int32),
            pltpu.SMEM((FR_DEV, 1, MAXB), jnp.int32),
            pltpu.SMEM((FR_DEV,), jnp.int32),
            pltpu.VMEM((FR_DEV, PB_DEV, PIX), jnp.float32),
            pltpu.VMEM((FR_DEV, PB_DEV, PIX), jnp.float32),
            pltpu.VMEM((SLOTS * PIX, VOX), jnp.bfloat16),
            pltpu.VMEM((FAR, 2 * FR_DEV * PB_DEV, PIX), jnp.bfloat16),
            pltpu.VMEM((near, 1, PIX), jnp.int32),
            pltpu.VMEM((near, message, PIX), jnp.bfloat16),
            pltpu.VMEM((near, message, PIX), jnp.bfloat16),
            pltpu.VMEM((2 * SLOTS, SLOTS * PIX), jnp.bfloat16),
            pltpu.VMEM((rows, 6 * SLOTS), jnp.bfloat16),
            pltpu.VMEM((HALVES, rows, WIDTH), jnp.float32),
            pltpu.VMEM((HALVES, 2 * groups * ROWS_DEV, WIDTH), jnp.int16),
            pltpu.VMEM((HALVES, groups, 2 * ROWS_DEV, WIDTH), jnp.int16),
            pltpu.VMEM((HALVES, groups, 2 * WIDTH // PIX, PIX), jnp.float32),
            pltpu.VMEM((HALVES, groups, 2 * WIDTH // PIX, PIX), jnp.float32),
            pltpu.VMEM((2, HALVES, 2 * WIDTH // PIX, PIX), jnp.float32),
            pltpu.VMEM((HALVES, groups, 2 * WIDTH // PIX, PIX), jnp.float32),
            dma((5,)),
            dma((CHUNKS,)),
            dma,
            dma,
            pltpu.SemaphoreType.REGULAR((2,)),
            dma,
            dma,
            dma,
            dma,
            dma((HALVES,)),
            dma((HALVES,)),
            dma((HALVES,)),
            dma((HALVES,)),
            dma((2,)),
            dma,
        ],
        compiler_params=pltpu.CompilerParams(
            collective_id=0, has_side_effects=True, vmem_limit_bytes=32 * 1024 * 1024
        ),
    )(
        *[
            pltpu.with_memory_space_constraint(x, pltpu.HBM)
            for x in (
                pix_index,
                vox_offset,
                block_count.reshape(FR_DEV),
                intensity,
                correction,
                splitting.reshape(SLOTS * PIX, VOX),
            )
        ]
    )
    weight = total[ROWS_DEV:]
    merged = total[:ROWS_DEV] / jnp.maximum(weight, 1.0)
    return (merged[None], weight[None])


def solution(mesh):
    placed = (
        P("frame", "brick", None),
        P("frame", "brick", None),
        P("frame", "brick", None, None, None),
        P("frame", "brick"),
        P("frame", "brick", None),
        P("frame", "brick", None),
    )
    return jax.shard_map(
        on_device,
        mesh=mesh,
        in_specs=placed,
        out_specs=(P("brick", "frame", None), P("brick", "frame", None)),
        check_vma=False,
    )
```

```python
import functools

import jax
import jax.numpy as jnp
from jax import lax
from jax.experimental import pallas as pl
from jax.experimental.pallas import tpu as pltpu
from jax.sharding import PartitionSpec as P

MESH = pl.DeviceIdType.MESH
CAP = 4
FR_DEV = 4
MAXB = 8
PB_DEV = 16
ROWS_DEV = 16
SLOTS = FR_DEV * MAXB
PIX = 128
VOX = 512
HALVES = 1
WIDTH = VOX // HALVES
CHUNKS = 4
LEVELS = 32767.0
FAR = 4


def iota(shape, dim):
    return lax.broadcasted_iota(jnp.int32, shape, dim)


def kernel(
    bricks,
    groups,
    pix_hbm,
    vox_hbm,
    count_hbm,
    intensity_hbm,
    correction_hbm,
    split_hbm,
    total,
    pix_ref,
    vox_ref,
    count_ref,
    inten,
    corr,
    split,
    pixels,
    request,
    packed,
    received,
    lhs,
    placer,
    acc,
    coded,
    partial,
    scale,
    scales,
    over_send,
    over_recv,
    load_sem,
    split_sem,
    pix_send,
    pix_recv,
    met,
    req_send,
    req_recv,
    data_send,
    data_recv,
    sum_send,
    sum_recv,
    scale_send,
    scale_recv,
    over_send_sem,
    over_sem,
):
    me_f = lax.axis_index("frame")
    me_b = lax.axis_index("brick")
    near = bricks // FAR
    me_y = me_b // (2 * FAR)
    me_c = lax.rem(me_b, 2)
    me_far = lax.rem(me_b // 2, FAR)
    me_near = me_y * 2 + me_c
    held = CAP * FAR
    barrier = pltpu.get_barrier_semaphore()

    def brick_peer(i):
        return lax.rem(me_b + i, bricks)

    def brick_of(at_near, at_far):
        return (at_near // 2 * FAR + at_far) * 2 + lax.rem(at_near, 2)

    order = sorted(range(1, near), key=lambda i: (-min(i, near - i), i))

    def near_index(i):
        return lax.rem(me_near + i, near)

    def near_peer(i):
        return brick_of(near_index(i), me_far)

    def far_peer(i):
        return brick_of(me_near, lax.rem(me_far + i, FAR))

    line = groups // 2
    me_line = me_f // line
    other_core = me_b + 1 - 2 * lax.rem(me_b, 2)

    def line_peer(i):
        return me_line * line + lax.rem(me_f + i, line)

    def frame_peer(i):
        return lax.rem(me_f + i, groups)

    for i in range(1, FAR):
        pl.semaphore_signal(
            barrier, inc=1, device_id={"brick": far_peer(i)}, device_id_type=MESH
        )
    for i in range(2, near, 2):
        pl.semaphore_signal(
            barrier, inc=1, device_id={"brick": near_peer(i)}, device_id_type=MESH
        )
    pl.semaphore_signal(barrier, inc=1, device_id={"brick": other_core}, device_id_type=MESH)
    for i in range(1, line):
        pl.semaphore_signal(
            barrier, inc=1, device_id={"frame": line_peer(i)}, device_id_type=MESH
        )
    pl.semaphore_signal(
        barrier, inc=1, device_id={"frame": frame_peer(line)}, device_id_type=MESH
    )

    @pl.when((me_f == 0) | (me_f == groups - 1))
    def _():
        for i in range(1, line):
            pl.semaphore_signal(
                barrier,
                inc=1,
                device_id={"frame": (1 - me_line) * line + lax.rem(me_f + i, line)},
                device_id_type=MESH,
            )

    tables = [
        pltpu.make_async_copy(pix_hbm, pix_ref, load_sem.at[0]),
        pltpu.make_async_copy(vox_hbm, vox_ref, load_sem.at[1]),
        pltpu.make_async_copy(count_hbm, count_ref, load_sem.at[2]),
    ]
    loads = [
        pltpu.make_async_copy(intensity_hbm, inten, load_sem.at[3]),
        pltpu.make_async_copy(correction_hbm, corr, load_sem.at[4]),
    ]
    depth = SLOTS * PIX // CHUNKS
    splits = [
        pltpu.make_async_copy(
            split_hbm.at[pl.ds(k * depth, depth)],
            split.at[pl.ds(k * depth, depth)],
            split_sem.at[k],
        )
        for k in range(CHUNKS)
    ]
    for copy in tables + loads + splits:
        copy.start()
    for copy in tables:
        copy.wait()

    lane = iota((1, PIX), 1)
    row = jnp.full((1, PIX), -1, jnp.int32)
    for s in range(SLOTS):
        row = jnp.where(lane == s, pix_ref[s // MAXB, 0, s % MAXB], row)
    sub2, lane2 = iota((SLOTS, PIX), 0), iota((SLOTS, PIX), 1)
    column = jnp.sum(
        jnp.where(sub2 == lane2, jnp.broadcast_to(row, (SLOTS, PIX)), 0), axis=1, keepdims=True
    )
    near_row = (row // (2 * FAR * PB_DEV)) * 2 + ((row >> 4) & 1)
    near_col = (column // (2 * FAR * PB_DEV)) * 2 + ((column >> 4) & 1)
    same = (jnp.broadcast_to(near_row, (SLOTS, PIX)) == near_col).astype(jnp.int32)
    rank_row = jnp.sum(jnp.where(sub2 < lane2, same, 0), axis=0, keepdims=True)
    rank_col = jnp.sum(jnp.where(lane2 < sub2, same, 0), axis=1, keepdims=True)
    where_row = ((row >> 5) & (FAR - 1)) * 128 + (lane >> 3) * PB_DEV + (row & 15)
    code = (near_row * held + rank_row) * 1024 + where_row
    request[me_near] = jnp.where(lane < SLOTS, code, -1)
    key = near_col * held + rank_col
    wide = iota((SLOTS, near * 2 * held), 1)
    pick = jnp.concatenate(
        [jnp.where(wide == key * 2 + c, 1.0, 0.0).astype(jnp.float32) for c in range(2)],
        axis=0,
    ).astype(jnp.bfloat16)

    inner = groups * ROWS_DEV
    rows = 2 * inner + 16
    pieces = 3
    wide_lane = iota((1, pieces * 2 * SLOTS), 1)
    voxel = jnp.full((1, pieces * 2 * SLOTS), -1, jnp.int32)
    for s in range(SLOTS):
        f, m = s // MAXB, s % MAXB
        offset = vox_ref[f, 0, m]
        target = jnp.where(offset == 0, inner, jnp.where(offset == inner + 1, inner + 1, offset - 1))
        target = jnp.where(m < count_ref[f], target, -1)
        voxel = jnp.where((wide_lane & (SLOTS - 1)) == s, target, voxel)
    down = iota((rows, pieces * 2 * SLOTS), 0)
    tail = down >= 2 * inner
    own_voxel = jnp.where(tail, inner + (down & 7), (down >> 5) * ROWS_DEV + (down & 15))
    own_channel = jnp.where(tail, (down >> 3) & 1, (down >> 4) & 1)
    channel = (iota((rows, pieces * 2 * SLOTS), 1) // SLOTS) & 1
    hit = (own_voxel == voxel) & (own_channel == channel)
    placer[...] = jnp.where(hit, 1.0, 0.0).astype(jnp.float32).astype(jnp.bfloat16)

    for copy in loads:
        copy.wait()
    pixels[me_far] = jnp.concatenate(
        [inten[...].reshape(FR_DEV * PB_DEV, PIX), corr[...].reshape(FR_DEV * PB_DEV, PIX)],
        axis=0,
    ).astype(jnp.bfloat16)

    ends = jnp.where((me_f == line - 1) | (me_f == line), 0, 1)
    pl.semaphore_wait(barrier, FAR - 1 + near // 2 - 1 + 1 + line - 1 + 1 + ends)
    pl.semaphore_signal(met.at[0], inc=1, device_id={"brick": other_core}, device_id_type=MESH)
    pl.semaphore_signal(
        met.at[1], inc=1, device_id={"frame": frame_peer(line)}, device_id_type=MESH
    )

    def push(i):
        pltpu.make_async_remote_copy(
            src_ref=pixels.at[me_far],
            dst_ref=pixels.at[me_far],
            send_sem=pix_send,
            recv_sem=pix_recv,
            device_id={"brick": far_peer(i)},
            device_id_type=MESH,
        ).start()

    for i in range(FAR - 1, 0, -1):

        @pl.when(me_far >= i)
        def _():
            push(FAR - i)

    for i in range(FAR - 1, 0, -1):

        @pl.when(me_far + i < FAR)
        def _():
            push(i)

    pl.semaphore_wait(met.at[0], 1)
    pl.semaphore_wait(met.at[1], 1)
    for i in order:
        pltpu.make_async_remote_copy(
            src_ref=request.at[me_near],
            dst_ref=request.at[me_near],
            send_sem=req_send,
            recv_sem=req_recv,
            device_id={"brick": near_peer(i)},
            device_id_type=MESH,
        ).start()

    def others_of(buffer, count, sem):
        others = buffer.at[pl.ds(0, count - 1)]
        return pltpu.make_async_copy(others, others, sem)

    others_of(request, near, req_recv).wait()

    asked = jnp.concatenate(
        [jnp.broadcast_to(request[d], (2 * held, PIX)) for d in range(near)], axis=0
    )
    place = lax.rem(iota((near * 2 * held, PIX), 0), 2 * held)
    wanted = (asked >> 10) == me_near * held + (place >> 1)
    found = jnp.sum(jnp.where(wanted, (asked & 1023) + 1, 0), axis=1, keepdims=True)
    spot = jnp.where(found > 0, found - 1 + (place[:, 0:1] & 1) * 64, -1)
    select = jnp.where(iota((near * 2 * held, FAR * PIX), 1) == spot, 1.0, 0.0)
    select = select.astype(jnp.float32).astype(jnp.bfloat16)

    others_of(pixels, FAR, pix_recv).wait()
    blocks = jnp.dot(
        select, pixels[...].reshape(FAR * PIX, PIX), preferred_element_type=jnp.float32
    ).astype(jnp.bfloat16)
    packed[...] = blocks.reshape(near, 2 * held, PIX)

    for i in order:
        pltpu.make_async_remote_copy(
            src_ref=packed.at[near_index(i)],
            dst_ref=received.at[me_near],
            send_sem=data_send,
            recv_sem=data_recv,
            device_id={"brick": near_peer(i)},
            device_id_type=MESH,
        ).start()
    received[me_near] = packed[me_near]
    others_of(received, near, data_recv).wait()

    rows_of = jnp.dot(
        pick, received[...].reshape(near * 2 * held, PIX), preferred_element_type=jnp.float32
    ).astype(jnp.bfloat16)
    slot = iota((2 * SLOTS, PIX), 0) & (SLOTS - 1)
    for s in range(SLOTS):
        lhs[:, s * PIX : (s + 1) * PIX] = jnp.where(slot == s, rows_of, jnp.bfloat16(0.0))
    for copy in splits:
        copy.wait()

    def over_copy(side, half, step, owner):
        return pltpu.make_async_remote_copy(
            src_ref=over_send.at[side, half],
            dst_ref=over_recv.at[half, me_f],
            send_sem=over_send_sem.at[side],
            recv_sem=over_sem,
            device_id={"frame": owner, "brick": brick_peer(step)},
            device_id_type=MESH,
        )

    parts = WIDTH // PIX
    for half in range(HALVES):
        columns = pl.ds(half * WIDTH, WIDTH)
        contrib = jnp.dot(lhs[...], split[:, columns], preferred_element_type=jnp.float32)
        first = contrib.astype(jnp.bfloat16)
        left = contrib - first.astype(jnp.float32)
        second = left.astype(jnp.bfloat16)
        third = (left - second.astype(jnp.float32)).astype(jnp.bfloat16)
        acc[half] = jnp.dot(
            placer[...],
            jnp.concatenate([first, second, third], axis=0),
            preferred_element_type=jnp.float32,
        )

        for side in range(2):
            for c in range(2):
                for n in range(parts):
                    over_send[side, half, pl.ds(c * parts + n, 1), :] = acc[
                        half, pl.ds(2 * inner + c * 8 + side, 1), pl.ds(n * PIX, PIX)
                    ]

        @pl.when(me_b > 0)
        def _():
            over_copy(0, half, bricks - 1, groups - 1).start()

        @pl.when(me_b < bricks - 1)
        def _():
            over_copy(1, half, 1, 0).start()

        sums = acc[half, pl.ds(0, 2 * inner), :].reshape(2 * groups, ROWS_DEV, WIDTH)
        top = jnp.maximum(jnp.max(jnp.abs(sums), axis=1, keepdims=True), 1e-33)
        code = jnp.round(sums * (LEVELS / top)).astype(jnp.int32).astype(jnp.int16)
        coded[half] = code.reshape(2 * inner, WIDTH)
        top = top * (1.0 / LEVELS)
        for g in range(groups):
            for c in range(2):
                for n in range(parts):
                    scale[half, g, pl.ds(c * parts + n, 1), :] = top[
                        2 * g + c, :, n * PIX : (n + 1) * PIX
                    ]

        for i in range(1, groups):
            peer = frame_peer(i)
            pltpu.make_async_remote_copy(
                src_ref=scale.at[half, peer],
                dst_ref=scales.at[half, me_f],
                send_sem=scale_send.at[half],
                recv_sem=scale_recv.at[half],
                device_id={"frame": peer},
                device_id_type=MESH,
            ).start()
            pltpu.make_async_remote_copy(
                src_ref=coded.at[half, pl.ds(peer * 2 * ROWS_DEV, 2 * ROWS_DEV)],
                dst_ref=partial.at[half, me_f],
                send_sem=sum_send.at[half],
                recv_sem=sum_recv.at[half],
                device_id={"frame": peer},
                device_id_type=MESH,
            ).start()
        partial[half, me_f] = jnp.zeros((2 * ROWS_DEV, WIDTH), jnp.int16)
        scales[half, me_f] = jnp.zeros((2 * parts, PIX), jnp.float32)
        total[:, columns] = acc[
            half, pl.ds(pl.multiple_of(me_f * 2 * ROWS_DEV, 2 * ROWS_DEV), 2 * ROWS_DEV), :
        ]

    for half in range(HALVES):
        others = partial.at[half, pl.ds(0, groups - 1)]
        pltpu.make_async_copy(others, others, sum_recv.at[half]).wait()
        others = scales.at[half, pl.ds(0, groups - 1)]
        pltpu.make_async_copy(others, others, scale_recv.at[half]).wait()
        for c in range(2):
            for n in range(parts):
                where = (pl.ds(c * ROWS_DEV, ROWS_DEV), pl.ds(half * WIDTH + n * PIX, PIX))
                value = total[where]
                for g in range(groups):
                    term = partial[
                        half, g, pl.ds(c * ROWS_DEV, ROWS_DEV), pl.ds(n * PIX, PIX)
                    ]
                    value = value + term.astype(jnp.float32) * scales[half, g, pl.ds(c * parts + n, 1), :]
                total[where] = value

    def take_overhang(at):
        pltpu.make_async_copy(over_recv, over_recv, over_sem).wait()
        for half in range(HALVES):
            value = over_recv[half, 0]
            for g in range(1, groups):
                value = value + over_recv[half, g]
            for c in range(2):
                for n in range(parts):
                    where = (pl.ds(c * ROWS_DEV + at, 1), pl.ds(half * WIDTH + n * PIX, PIX))
                    total[where] = total[where] + value[c * parts + n : c * parts + n + 1]

    @pl.when((me_f == groups - 1) & (me_b < bricks - 1))
    def _():
        take_overhang(ROWS_DEV - 1)

    @pl.when((me_f == 0) & (me_b > 0))
    def _():
        take_overhang(0)

    others_of(pixels, FAR, pix_send).wait()
    others_of(request, near, req_send).wait()
    others_of(packed, near, data_send).wait()
    for half in range(HALVES):
        others = partial.at[half, pl.ds(0, groups - 1)]
        pltpu.make_async_copy(others, others, sum_send.at[half]).wait()
        others = scales.at[half, pl.ds(0, groups - 1)]
        pltpu.make_async_copy(others, others, scale_send.at[half]).wait()

    def sent_over(side):
        pltpu.make_async_copy(over_send.at[side], over_send.at[side], over_send_sem.at[side]).wait()

    @pl.when(me_b > 0)
    def _():
        sent_over(0)

    @pl.when(me_b < bricks - 1)
    def _():
        sent_over(1)


def on_device(intensity, correction, splitting, block_count, pix_index, vox_offset):
    bricks = lax.axis_size("brick")
    groups = lax.axis_size("frame")
    near = bricks // FAR
    message = 2 * CAP * FAR
    rows = 2 * groups * ROWS_DEV + 16
    hbm = pl.BlockSpec(memory_space=pltpu.HBM)
    dma = pltpu.SemaphoreType.DMA
    total = pl.pallas_call(
        functools.partial(kernel, bricks, groups),
        out_shape=jax.ShapeDtypeStruct((2 * ROWS_DEV, VOX), jnp.float32),
        in_specs=[hbm] * 6,
        out_specs=pl.BlockSpec(memory_space=pltpu.VMEM),
        scratch_shapes=[
            pltpu.SMEM((FR_DEV, 1, MAXB), jnp.int32),
            pltpu.SMEM((FR_DEV, 1, MAXB), jnp.int32),
            pltpu.SMEM((FR_DEV,), jnp.int32),
            pltpu.VMEM((FR_DEV, PB_DEV, PIX), jnp.float32),
            pltpu.VMEM((FR_DEV, PB_DEV, PIX), jnp.float32),
            pltpu.VMEM((SLOTS * PIX, VOX), jnp.bfloat16),
            pltpu.VMEM((FAR, 2 * FR_DEV * PB_DEV, PIX), jnp.bfloat16),
            pltpu.VMEM((near, 1, PIX), jnp.int32),
            pltpu.VMEM((near, message, PIX), jnp.bfloat16),
            pltpu.VMEM((near, message, PIX), jnp.bfloat16),
            pltpu.VMEM((2 * SLOTS, SLOTS * PIX), jnp.bfloat16),
            pltpu.VMEM((rows, 6 * SLOTS), jnp.bfloat16),
            pltpu.VMEM((HALVES, rows, WIDTH), jnp.float32),
            pltpu.VMEM((HALVES, 2 * groups * ROWS_DEV, WIDTH), jnp.int16),
            pltpu.VMEM((HALVES, groups, 2 * ROWS_DEV, WIDTH), jnp.int16),
            pltpu.VMEM((HALVES, groups, 2 * WIDTH // PIX, PIX), jnp.float32),
            pltpu.VMEM((HALVES, groups, 2 * WIDTH // PIX, PIX), jnp.float32),
            pltpu.VMEM((2, HALVES, 2 * WIDTH // PIX, PIX), jnp.float32),
            pltpu.VMEM((HALVES, groups, 2 * WIDTH // PIX, PIX), jnp.float32),
            dma((5,)),
            dma((CHUNKS,)),
            dma,
            dma,
            pltpu.SemaphoreType.REGULAR((2,)),
            dma,
            dma,
            dma,
            dma,
            dma((HALVES,)),
            dma((HALVES,)),
            dma((HALVES,)),
            dma((HALVES,)),
            dma((2,)),
            dma,
        ],
        compiler_params=pltpu.CompilerParams(
            collective_id=0, has_side_effects=True, vmem_limit_bytes=32 * 1024 * 1024
        ),
    )(
        *[
            pltpu.with_memory_space_constraint(x, pltpu.HBM)
            for x in (
                pix_index,
                vox_offset,
                block_count.reshape(FR_DEV),
                intensity,
                correction,
                splitting.reshape(SLOTS * PIX, VOX),
            )
        ]
    )
    weight = total[ROWS_DEV:]
    merged = total[:ROWS_DEV] / jnp.maximum(weight, 1.0)
    return (merged[None], weight[None])


def solution(mesh):
    placed = (
        P("frame", "brick", None),
        P("frame", "brick", None),
        P("frame", "brick", None, None, None),
        P("frame", "brick"),
        P("frame", "brick", None),
        P("frame", "brick", None),
    )
    return jax.shard_map(
        on_device,
        mesh=mesh,
        in_specs=placed,
        out_specs=(P("brick", "frame", None), P("brick", "frame", None)),
        check_vma=False,
    )
```
